32 devices in a mesh: grp: 2 (over y), az: 4 (over z), el: 2 (over x), fq: 2 (over core).
Axes of the slice: x: 2, y: 2, z: 4, core: 2. Of those that a mesh axis runs over, the one named last changes fastest.
Arguments:
- polar: bfloat16 [2, 64, 1024, 768], P(None, ('grp', 'el'), 'az', 'fq'), parts along dimension 1, may hold values from -6 to 6
- band_offset: int32 [1024, 768], P('az', 'fq'), may hold values from -8 to 5, as said below
- tap_count: int32 [1024, 768], P('az', 'fq'), may hold values from 4 to 8
- tap_weight: bfloat16 [8, 1024, 768], P(None, 'az', 'fq'), may hold values from -2.390625 to 2.390625
Outputs:
- image_out: bfloat16 [2, 64, 768, 1024], P(None, ('grp', 'el'), ('az', 'fq')), parts along dimension 1
The draws below stay inside these ranges and needn't reach their ends.
There are 2 independent parts, one for each index of `grp`. The reference program is written for one: setup_inputs(seed, part) draws one part's arguments, and reference() takes and returns one part's arrays. A program takes and returns all parts, laid end to end along the dimension named above; an argument that names none is the same for every part. Nothing has to cross between parts.
Inputs may be any that keep to these rules, and one draw needn't show every extreme that they name: band_offset[j, f] lies between -8 and 9 - tap_count[j, f], so a band reads azimuths j - 8 to j + 8; both ends are reached.
All inputs are finite; a program needn't handle non-finite values.
Results may differ from the reference program's by a relative error of at most 0.0074.
Values may be sent and summed in bfloat16 or wider, within the bound.
A program may use at most 128 MiB of HBM per device.

```python
import math
import jax
import jax.numpy as jnp
from jax import lax

F = 768
A = 1024
E = 32
HW = 8
KT = 8


def band_pair(key):
    base_key = jax.random.fold_in(key, 4711)
    sub_keys = jax.random.split(base_key, 3)
    tap_draw = jax.random.randint(sub_keys[0], (A * F,), KT // 2, KT + 1, dtype=jnp.int32)
    raw_draw = jax.random.randint(sub_keys[1], (A * F,), 0, 1 << 20, dtype=jnp.int32)
    spread = 2 * HW + 2 - tap_draw
    offsets = raw_draw % spread - HW
    chosen = jax.random.randint(sub_keys[2], (3,), 0, A * F, dtype=jnp.int32)
    tap_draw = tap_draw.at[chosen[0]].set(KT)
    offsets = offsets.at[chosen[0]].set(-HW)
    offsets = offsets.at[chosen[1]].set(-HW)
    tap_draw = tap_draw.at[chosen[2]].set(KT // 2)
    offsets = offsets.at[chosen[2]].set(HW + 1 - KT // 2)
    return (offsets.reshape(A, F), tap_draw.reshape(A, F))


def draw_band_offset(key, part):
    return band_pair(key)[0]


def draw_tap_count(key, part):
    return band_pair(key)[1]


def block_scale(stream_key, shape, cuts, low, top_value):
    def one(position, shards_of):
        steps = jax.random.uniform(jax.random.fold_in(jax.random.fold_in(stream_key, 6), position), (shards_of,), jnp.float32, low / len(cuts), top_value / len(cuts))
        return jnp.repeat(jnp.exp(steps), shape[position] // shards_of).reshape((-1,) + (1,) * (len(shape) - position - 1))

    level = one(*cuts[0])
    for cut in cuts[1:]:
        level = level * one(*cut)
    return level


def normal_values(stream_key, dims, scale, bound, cuts=(), kind=jnp.bfloat16):
    array = jax.random.normal(stream_key, dims, jnp.float32) * scale
    if len(cuts) > 0:
        array = block_scale(stream_key, dims, cuts, -0.22, 0.18) * array
    return jnp.clip(array, min=-bound, max=bound).astype(kind)


def setup_inputs(seed: int = 0, part: int = 0) -> dict:
    streams_of = jax.random.split(jax.random.key(seed), 5)
    own_keys = jax.random.split(jax.random.fold_in(streams_of[4], part), 5)
    polar = normal_values(own_keys[0], (2, E, A, F), 1.0, 6.0, ((1, 2), (2, 4), (3, 2)))
    band_offset = draw_band_offset(jax.random.fold_in(streams_of[4], 71), part)
    tap_count = draw_tap_count(jax.random.fold_in(streams_of[4], 71), part)
    tap_weight = normal_values(streams_of[3], (KT, A, F), 0.4, 2.390625, ((1, 4), (2, 2)))
    return {"polar": polar, "band_offset": band_offset, "tap_count": tap_count, "tap_weight": tap_weight}


def table_pair(row_ids, col_ids, length):
    product = row_ids[:, None] * col_ids[None, :] % length
    angle = product.astype(jnp.float32) * (2.0 * math.pi / length)
    return (jnp.cos(angle).astype(jnp.bfloat16), jnp.sin(angle).astype(jnp.bfloat16))

def complex_dot(real_in, imag_in, cos_tab, sin_tab):
    real_wide = real_in.astype(jnp.float32)
    imag_wide = imag_in.astype(jnp.float32)
    cos_wide = cos_tab.astype(jnp.float32)
    sin_wide = sin_tab.astype(jnp.float32)
    high = lax.Precision.HIGHEST
    real_out = jnp.dot(real_wide, cos_wide, precision=high) - jnp.dot(imag_wide, sin_wide, precision=high)
    imag_out = jnp.dot(real_wide, sin_wide, precision=high) + jnp.dot(imag_wide, cos_wide, precision=high)
    return (real_out, imag_out)

def reference(polar, band_offset, tap_count, tap_weight):
    freq_ids = jnp.arange(F, dtype=jnp.int32)
    azim_ids = jnp.arange(A, dtype=jnp.int32)
    elev_ids = jnp.arange(E, dtype=jnp.int32)
    cos_f, sin_f = table_pair(freq_ids, freq_ids, F)
    cos_a, sin_a = table_pair(azim_ids, azim_ids, A)
    cos_e, sin_e = table_pair(elev_ids, elev_ids, E)
    weights = tap_weight.astype(jnp.float32)
    column_ids = azim_ids[:, None]

    def one_cut(cut_slab):
        padded = jnp.pad(cut_slab.astype(jnp.float32), ((0, 0), (HW, HW), (0, 0)))
        accumulated = jnp.zeros((2, A, F), jnp.float32)
        for tap_index in range(KT):
            source_index = jnp.minimum(column_ids + HW + band_offset + tap_index, A + 2 * HW - 1).astype(jnp.int32)
            gathered = jnp.take_along_axis(padded, jnp.broadcast_to(source_index[None], (2, A, F)), axis=1)
            accumulated = accumulated + jnp.where((tap_index < tap_count)[None], weights[tap_index][None] * gathered, 0.0)
        interpolated = accumulated.astype(jnp.bfloat16)
        range_real, range_imag = complex_dot(interpolated[0], interpolated[1], cos_f, sin_f)
        ranged = (jnp.stack([range_real, range_imag]) * (1.0 / math.sqrt(F))).astype(jnp.bfloat16)
        transposed = jnp.swapaxes(ranged, 1, 2)
        cross_real, cross_imag = complex_dot(transposed[0], transposed[1], cos_a, sin_a)
        return (jnp.stack([cross_real, cross_imag]) * (1.0 / math.sqrt(A))).astype(jnp.bfloat16)
    crossed = lax.map(one_cut, jnp.moveaxis(polar, 1, 0))
    flattened = crossed.astype(jnp.float32).reshape(E, 2, F * A)
    cos_wide = cos_e.astype(jnp.float32)
    sin_wide = sin_e.astype(jnp.float32)
    high = lax.Precision.HIGHEST
    height_real = jnp.einsum('eh,ex->hx', cos_wide, flattened[:, 0], precision=high) - jnp.einsum('eh,ex->hx', sin_wide, flattened[:, 1], precision=high)
    height_imag = jnp.einsum('eh,ex->hx', sin_wide, flattened[:, 0], precision=high) + jnp.einsum('eh,ex->hx', cos_wide, flattened[:, 1], precision=high)
    image_out = (jnp.stack([height_real, height_imag]) * (1.0 / math.sqrt(E))).astype(jnp.bfloat16)
    return image_out.reshape(2, E, F, A)
```

```python
import math

import jax
import jax.numpy as jnp
from jax import lax
from jax.experimental import pallas as pl
from jax.experimental.pallas import tpu as pltpu
from jax.sharding import PartitionSpec as P

F = 768
A = 1024
E = 32
HW = 8
KT = 8
LANES = 128
GROUP = 16
TAPS = 2 * HW + 1
BATCH = 4
LATE = 4
SLOTS = 4
FIRST = 2
SPLIT = 2
TILE = 256
MESH = pl.DeviceIdType.MESH


def with_halo(cells, sides, width):
    for axis, dim in sides:
        count = lax.axis_size(axis)
        ends = count - 1
        head = lax.slice_in_dim(cells, 0, width, axis=dim)
        tail = lax.slice_in_dim(cells, cells.shape[dim] - width, cells.shape[dim], axis=dim)
        cells = jnp.concatenate(
            [
                lax.ppermute(tail, axis, [(i, (i + 1) % count) for i in range(ends)]),
                cells,
                lax.ppermute(head, axis, [((i + 1) % count, i) for i in range(ends)]),
            ],
            axis=dim,
        )
    return cells


def table_pair(row_ids, col_ids, length):
    product = row_ids[:, None] * col_ids[None, :] % length
    angle = product.astype(jnp.float32) * (2.0 * math.pi / length)
    return (jnp.cos(angle).astype(jnp.bfloat16), jnp.sin(angle).astype(jnp.bfloat16))


def on_device(polar, band_offset, tap_count, tap_weight):
    shape_all = polar.shape
    col_count = shape_all[2]
    freq_count = shape_all[3]
    az_count = lax.axis_size("az")
    fq_count = lax.axis_size("fq")
    el_count = lax.axis_size("el")
    padded = with_halo(polar, (("az", 2),), HW)
    window = col_count + 2 * HW
    column = jnp.arange(col_count, dtype=jnp.int32)[:, None]
    position = jnp.arange(window, dtype=jnp.int32)[None, :, None]
    band_matrix = jnp.zeros((col_count, window, freq_count), jnp.bfloat16)
    for tap_index in range(KT):
        reach = column + HW + band_offset + tap_index
        matches = (position == reach[:, None, :]) & (tap_index < tap_count)[:, None, :]
        band_matrix = jnp.where(matches, tap_weight[tap_index][:, None, :], band_matrix)
    interpolated = jnp.einsum(
        "jaf,ceaf->cejf", band_matrix, padded, preferred_element_type=jnp.float32
    ).astype(jnp.bfloat16)
    fq_index = lax.axis_index("fq")
    bin_count = F // (fq_count * az_count)
    az_block = jnp.arange(az_count, dtype=jnp.int32)[:, None]
    bin_local = jnp.arange(bin_count, dtype=jnp.int32)[None, :]
    range_bins = ((az_block * fq_count + fq_index) * bin_count + bin_local).reshape(-1)
    cos_f, sin_f = table_pair(jnp.arange(F, dtype=jnp.int32), range_bins, F)
    shard_piece = lax.all_gather(interpolated, "fq", axis=3, tiled=True)
    cos_rows = cos_f
    sin_rows = sin_f
    real_part = jnp.einsum(
        "ejf,fk->ekj", shard_piece[0], cos_rows, preferred_element_type=jnp.float32
    ) - jnp.einsum("ejf,fk->ekj", shard_piece[1], sin_rows, preferred_element_type=jnp.float32)
    imag_part = jnp.einsum(
        "ejf,fk->ekj", shard_piece[0], sin_rows, preferred_element_type=jnp.float32
    ) + jnp.einsum("ejf,fk->ekj", shard_piece[1], cos_rows, preferred_element_type=jnp.float32)
    summed = jnp.stack([real_part, imag_part])
    ranged = (summed * (1.0 / math.sqrt(F))).astype(jnp.bfloat16)
    azim_ids = jnp.arange(A, dtype=jnp.int32)
    cos_a, sin_a = table_pair(azim_ids, azim_ids, A)
    block_data = lax.all_to_all(ranged, "az", split_axis=2, concat_axis=3, tiled=True)
    real_part = jnp.einsum(
        "ekj,jm->ekm", block_data[0], cos_a, preferred_element_type=jnp.float32
    ) - jnp.einsum("ekj,jm->ekm", block_data[1], sin_a, preferred_element_type=jnp.float32)
    imag_part = jnp.einsum(
        "ekj,jm->ekm", block_data[0], sin_a, preferred_element_type=jnp.float32
    ) + jnp.einsum("ekj,jm->ekm", block_data[1], cos_a, preferred_element_type=jnp.float32)
    crossed = (jnp.stack([real_part, imag_part]) * (1.0 / math.sqrt(A))).astype(jnp.bfloat16)
    elev_ids = jnp.arange(E, dtype=jnp.int32)
    el_index = lax.axis_index("el")
    height_count = E // el_count
    height_rows = el_index * height_count + jnp.arange(height_count, dtype=jnp.int32)
    cos_e, sin_e = table_pair(elev_ids, height_rows, E)
    shard_piece = lax.all_gather(crossed, "el", axis=1, tiled=True)
    cos_rows = cos_e
    sin_rows = sin_e
    real_part = jnp.einsum(
        "eh,ekm->hkm", cos_rows, shard_piece[0], preferred_element_type=jnp.float32
    ) - jnp.einsum("eh,ekm->hkm", sin_rows, shard_piece[1], preferred_element_type=jnp.float32)
    imag_part = jnp.einsum(
        "eh,ekm->hkm", sin_rows, shard_piece[0], preferred_element_type=jnp.float32
    ) + jnp.einsum("eh,ekm->hkm", cos_rows, shard_piece[1], preferred_element_type=jnp.float32)
    totals = jnp.stack([real_part, imag_part])
    image_out = (totals * (1.0 / math.sqrt(E))).astype(jnp.bfloat16)
    return image_out


def small_trig(product, length):
    value = product.astype(jnp.float32)
    turns = jnp.floor(value * (1.0 / length))
    angle = (value - turns * length) * (2.0 * math.pi / length)
    return jnp.cos(angle), jnp.sin(angle)


def iota(shape, dim):
    return lax.broadcasted_iota(jnp.int32, shape, dim)


def fused_body(
    polar, off_h, cnt_h, tap_h, out_h,
    xs, buf, pv, wt, offv, cntv, tapv, hl, hr,
    lowc, lows, highc, highs, rtab, cos_a, sin_a, htab,
    rl, zl, er, eh, ez, ch, ost, est,
    in_sem, pv_sem, halo_s, halo_r, fq_s, fq_r, zl_s, zl_r,
    xe_s, xe_r, ze_s, ze_r, xa_s, xa_r, xb_s, xb_r, lo_sem, eo_sem,
):
    n_az = lax.axis_size("az")
    az, fq, el = (lax.axis_index(name) for name in ("az", "fq", "el"))
    _, cuts, cols, freqs = polar.shape
    parts = freqs // LANES
    heights = E // 2
    late = LATE * GROUP
    bins = out_h.shape[2]
    early_groups = (bins - late) // GROUP
    batches = cuts // BATCH
    steps = cols // GROUP

    def at_az(shift):
        return {"az": lax.rem(az + shift, n_az)}

    def lane_block(index, size):
        return pl.ds(pl.multiple_of(index * size, LANES), size)

    fq_peer = {"fq": 1 - fq}
    el_peer = {"el": 1 - el}
    own_cols = lane_block(az, cols)

    def from_az(shift):
        return lane_block(lax.rem(az - shift + n_az, n_az), cols)

    def remote(source, target, send, recv, where):
        return pltpu.make_async_remote_copy(
            src_ref=source,
            dst_ref=target,
            send_sem=send,
            recv_sem=recv,
            device_id=where,
            device_id_type=MESH,
        )

    def polar_copy(c):
        slot = lax.rem(c, SLOTS)
        return pltpu.make_async_copy(polar.at[:, c], pv.at[slot], pv_sem.at[slot])

    spans = (pl.ds(0, FIRST), pl.ds(FIRST, cuts - FIRST))

    def halo_up(k):
        return remote(
            polar.at[:, spans[k], pl.ds(cols - HW, HW)],
            hl.at[:, spans[k]],
            halo_s.at[0, k],
            halo_r.at[0, k],
            at_az(1),
        )

    def halo_down(k):
        return remote(
            polar.at[:, spans[k], pl.ds(0, HW)],
            hr.at[:, spans[k]],
            halo_s.at[1, k],
            halo_r.at[1, k],
            at_az(n_az - 1),
        )

    def fq_copy(c, lanes):
        return remote(
            xs.at[c, :, :, lanes], xs.at[c, :, :, lanes], fq_s.at[c], fq_r.at[c], fq_peer
        )

    def zl_copy(c, shift, lanes):
        return remote(
            rl.at[c, shift - 1],
            zl.at[c // BATCH, :, lax.rem(c, BATCH), :, lanes],
            zl_s.at[c, shift - 1],
            zl_r.at[c, shift - 1],
            at_az(shift),
        )

    def xe_copy(c):
        return remote(
            er.at[:, :, 0, :, c], er.at[:, :, 1, :, c], xe_s.at[c], xe_r.at[c], el_peer
        )

    def ze_copy(g, q, shift, lanes):
        span = pl.ds(q * (heights // SPLIT), heights // SPLIT)
        return remote(
            eh.at[g, shift - 1, :, span],
            ez.at[g, :, span, :, lanes],
            ze_s.at[g, q, shift - 1],
            ze_r.at[g, q, shift - 1],
            at_az(shift),
        )

    def xa_copy(b):
        span = pl.ds(b * BATCH, BATCH)
        return remote(
            ch.at[:, 0, :, span], ch.at[:, 1, :, span], xa_s.at[b], xa_r.at[b], el_peer
        )

    def xb_copy(b, g):
        span = pl.ds(b * BATCH, BATCH)
        half = batches // 2
        return remote(
            ch.at[g, 0, :, span],
            ch.at[g, 1, :, span],
            xb_s.at[b - half, g],
            xb_r.at[b - half, g],
            el_peer,
        )

    barrier = pltpu.get_barrier_semaphore()
    peers = [fq_peer, el_peer] + [at_az(s) for s in range(1, n_az)]
    for peer in peers:
        pl.semaphore_signal(barrier, inc=1, device_id=peer, device_id_type=MESH)
    loads = [
        pltpu.make_async_copy(off_h, offv, in_sem.at[0]),
        pltpu.make_async_copy(cnt_h, cntv, in_sem.at[1]),
        pltpu.make_async_copy(tap_h, tapv, in_sem.at[2]),
    ]
    for load in loads:
        load.start()
    for c in range(SLOTS):
        polar_copy(c).start()

    @pl.when(az == 0)
    def _():
        hl[...] = jnp.zeros(hl.shape, hl.dtype)

    @pl.when(az == n_az - 1)
    def _():
        hr[...] = jnp.zeros(hr.shape, hr.dtype)

    pl.semaphore_wait(barrier, len(peers))

    @pl.when(az < n_az - 1)
    def _():
        for k in range(2):
            halo_up(k).start()

    @pl.when(az > 0)
    def _():
        for k in range(2):
            halo_down(k).start()

    block = 32
    blocks = n_az * bins // block
    per = bins // block
    row = iota((16, F), 0)
    shift = jnp.zeros((16, F), jnp.int32)
    for s in range(1, n_az):
        shift = shift + (row >= s * per).astype(jnp.int32)
    inner = row - shift * per
    target = az + shift
    target = jnp.where(target >= n_az, target - n_az, target)
    starts = (target * 2 + fq) * bins + inner * block
    wide = slice(0, F)
    highc[0:16, wide], highs[0:16, wide] = small_trig(starts * iota((16, F), 1), F)
    lowc[:, wide], lows[:, wide] = small_trig(iota((block, F), 0) * iota((block, F), 1), F)

    @pl.loop(0, blocks)
    def _(i):
        hc, hs = highc[pl.ds(i, 1), wide], highs[pl.ds(i, 1), wide]
        lc, ls = lowc[:, wide], lows[:, wide]
        at = pl.ds(pl.multiple_of(i * block, block), block)
        rtab[at, :] = (hc * lc - hs * ls).astype(jnp.bfloat16)
        at = pl.ds(pl.multiple_of((blocks + i) * block, block), block)
        rtab[at, :] = (hs * lc + hc * ls).astype(jnp.bfloat16)

    for load in loads:
        load.wait()

    @pl.loop(0, parts * steps)
    def _(i):
        g = i // steps
        rows = pl.ds(pl.multiple_of(lax.rem(i, steps) * GROUP, GROUP), GROUP)
        lanes = lane_block(g, LANES)
        rel = offv[rows, lanes] + HW
        cnt = cntv[rows, lanes]
        zero = jnp.zeros(rel.shape, jnp.float32)
        taps = [
            jnp.where(t < cnt, tapv[t, rows, lanes].astype(jnp.float32), zero)
            for t in range(KT)
        ]
        for bit in range(4):
            step = 1 << bit
            on = (rel & step) != 0
            size = min(TAPS, len(taps) + step)
            taps = [
                jnp.where(
                    on,
                    taps[d - step] if d >= step else zero,
                    taps[d] if d < len(taps) else zero,
                )
                for d in range(size)
            ]
        for d in range(TAPS):
            wt[d, g, rows, :] = taps[d]

    def wait_halo(k):
        @pl.when(az > 0)
        def _():
            halo_up(k).wait_recv()

        @pl.when(az < n_az - 1)
        def _():
            halo_down(k).wait_recv()

    def interpolate(c):
        slot = lax.rem(c, SLOTS)
        polar_copy(c).wait()

        @pl.when(c == 0)
        def _():
            wait_halo(0)

        @pl.when(c == FIRST)
        def _():
            wait_halo(1)

        for p in range(2):
            for g in range(parts):
                lanes = slice(g * LANES, (g + 1) * LANES)
                buf[p, g, 0:HW, :] = hl[p, c, :, lanes].astype(jnp.float32)
                buf[p, g, HW : HW + cols, :] = pv[slot, p, :, lanes].astype(jnp.float32)
                buf[p, g, HW + cols :, :] = hr[p, c, :, lanes].astype(jnp.float32)

        @pl.loop(0, parts * steps)
        def _(i):
            g = i // steps
            base = pl.multiple_of(lax.rem(i, steps) * GROUP, GROUP)
            lanes = lane_block(fq * parts + g, LANES)
            weights = [wt[d, g, pl.ds(base, GROUP), :] for d in range(TAPS)]
            for p in range(2):
                acc = [None, None]
                for o in range(TAPS + 8):
                    cell = buf[p, g, pl.ds(base + o, 8), :]
                    for v in range(2):
                        d = o - 8 * v
                        if 0 <= d < TAPS:
                            term = weights[d][8 * v : 8 * v + 8] * cell
                            acc[v] = term if acc[v] is None else acc[v] + term
                value = jnp.concatenate(acc, axis=0).astype(jnp.bfloat16)
                xs[c, p, pl.ds(base, GROUP), lanes] = value

        fq_copy(c, lane_block(fq, freqs)).start()

        @pl.when(c + SLOTS < cuts)
        def _():
            polar_copy(c + SLOTS).start()

    def range_step(c):
        fq_copy(c, lane_block(1 - fq, freqs)).wait_recv()
        dims = (((1,), (1,)), ((), ()))
        table = rtab[...]
        fr = lax.dot_general(table, xs[c, 0], dims, preferred_element_type=jnp.float32)
        fi = lax.dot_general(table, xs[c, 1], dims, preferred_element_type=jnp.float32)
        half = n_az * bins
        scale = 1.0 / math.sqrt(F)
        real = ((fr[:half] - fi[half:]) * scale).astype(jnp.bfloat16)
        imag = ((fr[half:] + fi[:half]) * scale).astype(jnp.bfloat16)
        b, k = c // BATCH, lax.rem(c, BATCH)
        for p, part in enumerate((real, imag)):
            for s in range(n_az):
                piece = part[s * bins : s * bins + late]
                if s == 0:
                    zl[b, p, k, :, own_cols] = piece
                else:
                    rl[c, s - 1, p] = piece
                for g in range(early_groups):
                    at = s * bins + late + g * GROUP
                    er[g, s, 0, p, c] = part[at : at + GROUP]
        for s in order:
            zl_copy(c, s, own_cols).start()
        xe_copy(c).start()

    middle = n_az // 2
    order = [middle] + [s for s in range(1, n_az) if s != middle]

    def azimuth_tables():
        size = 1024 // block
        col = iota((block, A), 1)
        lowc[...], lows[...] = small_trig(iota((block, A), 0) * col, A)
        highc[...], highs[...] = small_trig(iota((A // block, A), 0) * block * col, A)

        @pl.loop(0, A // block)
        def _(i):
            hc, hs = highc[pl.ds(i, 1), :], highs[pl.ds(i, 1), :]
            at = pl.ds(pl.multiple_of(i * block, block), block)
            cos_a[at, :] = (hc * lowc[...] - hs * lows[...]).astype(jnp.bfloat16)
            sin_a[at, :] = (hs * lowc[...] + hc * lows[...]).astype(jnp.bfloat16)

    def height_tables():
        rows, width = 2 * heights, 4 * cuts
        row, col = iota((rows, 128), 0), iota((rows, 128), 1)
        out_imag = row >= heights
        height = el * heights + jnp.where(out_imag, row - heights, row)
        other = col >= 2 * cuts
        inner = jnp.where(other, col - 2 * cuts, col)
        in_imag = inner >= cuts
        source = jnp.where(other, 1 - el, el)
        elev = source * cuts + jnp.where(in_imag, inner - cuts, inner)
        cos_e, sin_e = small_trig(height * elev, E)
        sign = jnp.where(out_imag, sin_e, -sin_e)
        small = jnp.where(out_imag == in_imag, cos_e, sign)
        small = jnp.where(col < width, small, 0.0).astype(jnp.bfloat16)
        tall = rows * GROUP
        take_row = (iota((tall, rows), 0) // GROUP == iota((tall, rows), 1)).astype(
            jnp.bfloat16
        )
        mid = jnp.dot(take_row, small, preferred_element_type=jnp.float32)
        mid = mid.astype(jnp.bfloat16)

        @pl.loop(0, width * GROUP // TILE)
        def _(i):
            shape = (128, TILE)
            col_at = iota(shape, 1) + i * TILE
            take_col = (iota(shape, 0) == col_at // GROUP).astype(jnp.bfloat16)
            spread = jnp.dot(mid, take_col, preferred_element_type=jnp.float32)
            shape = (tall, TILE)
            same = (iota(shape, 0) & (GROUP - 1)) == (iota(shape, 1) & (GROUP - 1))
            htab[:, lane_block(i, TILE)] = jnp.where(same, spread, 0.0).astype(jnp.bfloat16)

    def cross_tile(left, t):
        rows = left.shape[0] // 2
        scale = 1.0 / math.sqrt(A)
        by_cos = jnp.dot(left, cos_a[:, lane_block(t, TILE)], preferred_element_type=jnp.float32)
        by_sin = jnp.dot(left, sin_a[:, lane_block(t, TILE)], preferred_element_type=jnp.float32)
        real = ((by_cos[:rows] - by_sin[rows:]) * scale).astype(jnp.bfloat16)
        imag = ((by_sin[:rows] + by_cos[rows:]) * scale).astype(jnp.bfloat16)
        return real, imag

    def cross_late(b):
        for k in range(BATCH):
            for s in order:
                zl_copy(b * BATCH + k, s, from_az(s)).wait_recv()

        @pl.loop(0, A // TILE)
        def _(t):
            left = zl[b].reshape(2 * BATCH * late, A)
            for p, part in enumerate(cross_tile(left, t)):
                part = part.reshape(BATCH, LATE, GROUP, TILE)
                for g in range(LATE):
                    span = pl.ds(b * BATCH, BATCH)
                    ch[g, 0, p, span, :, lane_block(t, TILE)] = part[:, g]

    def early_heights(g):
        @pl.loop(0, n_az)
        def _(s):
            data = er[g, s].reshape(4 * cuts * GROUP, cols)
            total = jnp.dot(htab[...], data, preferred_element_type=jnp.float32)
            total = (total * (1.0 / math.sqrt(E))).astype(jnp.bfloat16)
            total = total.reshape(2, heights, GROUP, cols)

            @pl.when(s == 0)
            def _():
                ez[g, :, :, :, own_cols] = total

            @pl.when(s > 0)
            def _():
                eh[g, s - 1] = total

        for q in range(SPLIT):
            for s in order:
                ze_copy(g, q, s, own_cols).start()

    def early_out(g, q):
        span = pl.ds(q * (heights // SPLIT), heights // SPLIT)
        return pltpu.make_async_copy(
            est.at[g, q],
            out_h.at[:, span, pl.ds(late + g * GROUP, GROUP), :],
            eo_sem.at[g, q],
        )

    def cross_early(g, q):
        for s in order:
            ze_copy(g, q, s, from_az(s)).wait_recv()
        some = heights // SPLIT

        @pl.loop(0, A // TILE)
        def _(t):
            left = ez[g, :, q * some : (q + 1) * some].reshape(2 * some * GROUP, A)
            for p, part in enumerate(cross_tile(left, t)):
                est[g, q, p, :, :, lane_block(t, TILE)] = part.reshape(some, GROUP, TILE)

        early_out(g, q).start()

    def late_out(g):
        return pltpu.make_async_copy(
            ost.at[g % 2], out_h.at[:, :, pl.ds(g * GROUP, GROUP), :], lo_sem.at[g]
        )

    def late_heights(g):
        if g == 0:
            for b in range(batches // 2):
                xa_copy(b).wait_recv()
        for b in range(batches // 2, batches):
            xb_copy(b, g).wait_recv()
        if g >= 2:
            late_out(g - 2).wait()

        @pl.loop(0, A // TILE)
        def _(t):
            at = lane_block(t, TILE)
            data = ch[g, :, :, :, :, at].reshape(4 * cuts * GROUP, TILE)
            total = jnp.dot(htab[...], data, preferred_element_type=jnp.float32)
            total = (total * (1.0 / math.sqrt(E))).astype(jnp.bfloat16)
            ost[g % 2, :, :, :, at] = total.reshape(2, heights, GROUP, TILE)

        late_out(g).start()

    def front(first, last):
        @pl.loop(first, last)
        def _(c):
            @pl.when(c < cuts)
            def _():
                interpolate(c)

            @pl.when(c > 0)
            def _():
                range_step(c - 1)

    pause = cuts // 2 + 2
    front(0, pause)
    azimuth_tables()
    height_tables()
    cross_late(0)
    xa_copy(0).start()
    front(pause, cuts + 1)
    cross_late(1)
    xa_copy(1).start()
    cross_late(2)
    xb_copy(2, 0).start()
    xb_copy(2, 1).start()
    for c in range(cuts):
        xe_copy(c).wait_recv()
    for g in range(early_groups):
        early_heights(g)
    cross_late(3)
    for b, g in ((3, 0), (3, 1), (2, 2), (3, 2), (2, 3), (3, 3)):
        xb_copy(b, g).start()
    cross_early(0, 0)
    late_heights(0)
    cross_early(0, 1)
    late_heights(1)
    cross_early(1, 0)
    late_heights(2)
    cross_early(1, 1)
    late_heights(3)

    @pl.when(az < n_az - 1)
    def _():
        for k in range(2):
            halo_up(k).wait_send()

    @pl.when(az > 0)
    def _():
        for k in range(2):
            halo_down(k).wait_send()

    @pl.loop(0, cuts)
    def _(c):
        fq_copy(c, lane_block(fq, freqs)).wait_send()
        for s in order:
            zl_copy(c, s, own_cols).wait_send()
        xe_copy(c).wait_send()

    for g in range(early_groups):
        for q in range(SPLIT):
            for s in order:
                ze_copy(g, q, s, own_cols).wait_send()
    for b in range(batches // 2):
        xa_copy(b).wait_send()
    for b in range(batches // 2, batches):
        for g in range(LATE):
            xb_copy(b, g).wait_send()
    for g in range(early_groups):
        for q in range(SPLIT):
            early_out(g, q).wait()
    for g in range(LATE - 2, LATE):
        late_out(g).wait()


def fused(polar, band_offset, tap_count, tap_weight):
    _, cuts, cols, freqs = polar.shape
    n_az = lax.axis_size("az")
    bins = F // (2 * n_az)
    late = LATE * GROUP
    heights = E // 2
    parts = freqs // LANES
    groups = (bins - late) // GROUP
    batches = cuts // BATCH
    far = n_az - 1
    half = jnp.bfloat16
    vmem = pltpu.VMEM
    dma = pltpu.SemaphoreType.DMA
    return pl.pallas_call(
        fused_body,
        out_shape=jax.ShapeDtypeStruct((2, heights, bins, A), half),
        in_specs=[pl.BlockSpec(memory_space=pl.ANY)] * 4,
        out_specs=pl.BlockSpec(memory_space=pl.ANY),
        scratch_shapes=[
            vmem((cuts, 2, cols, F), half),
            vmem((2, parts, cols + 2 * HW, LANES), jnp.float32),
            vmem((SLOTS, 2, cols, freqs), half),
            vmem((TAPS, parts, cols, LANES), jnp.float32),
            vmem((cols, freqs), jnp.int32),
            vmem((cols, freqs), jnp.int32),
            vmem((KT, cols, freqs), half),
            vmem((2, cuts, HW, freqs), half),
            vmem((2, cuts, HW, freqs), half),
            vmem((32, A), jnp.float32),
            vmem((32, A), jnp.float32),
            vmem((32, A), jnp.float32),
            vmem((32, A), jnp.float32),
            vmem((2 * n_az * bins, F), half),
            vmem((A, A), half),
            vmem((A, A), half),
            vmem((2 * heights * GROUP, 4 * cuts * GROUP), half),
            vmem((cuts, far, 2, late, cols), half),
            vmem((batches, 2, BATCH, late, A), half),
            vmem((groups, n_az, 2, 2, cuts, GROUP, cols), half),
            vmem((groups, far, 2, heights, GROUP, cols), half),
            vmem((groups, 2, heights, GROUP, A), half),
            vmem((LATE, 2, 2, cuts, GROUP, A), half),
            vmem((2, 2, heights, GROUP, A), half),
            vmem((groups, SPLIT, 2, heights // SPLIT, GROUP, A), half),
            dma((3,)),
            dma((SLOTS,)),
            dma((2, 2)),
            dma((2, 2)),
            dma((cuts,)),
            dma((cuts,)),
            dma((cuts, far)),
            dma((cuts, far)),
            dma((cuts,)),
            dma((cuts,)),
            dma((groups, SPLIT, far)),
            dma((groups, SPLIT, far)),
            dma((batches // 2,)),
            dma((batches // 2,)),
            dma((batches // 2, LATE)),
            dma((batches // 2, LATE)),
            dma((LATE,)),
            dma((groups, SPLIT)),
        ],
        compiler_params=pltpu.CompilerParams(
            collective_id=0, has_side_effects=True, vmem_limit_bytes=67043328
        ),
        name="image",
    )(polar, band_offset, tap_count, tap_weight)


def pick(polar, band_offset, tap_count, tap_weight):
    _, e_here, col_count, freq_count = polar.shape
    az_count = lax.axis_size("az")
    bins = F // (lax.axis_size("fq") * az_count)
    fits = (
        lax.axis_size("fq") == 2
        and lax.axis_size("el") == 2
        and az_count == 4
        and e_here == 4 * BATCH
        and bins == (LATE + 2) * GROUP
        and col_count == TILE
        and freq_count % LANES == 0
    )
    run = fused if fits else on_device
    return run(polar, band_offset, tap_count, tap_weight)


def solution(mesh):
    in_specs = (
        P(None, ("grp", "el"), "az", "fq"),
        P("az", "fq"),
        P("az", "fq"),
        P(None, "az", "fq"),
    )
    out_specs = P(None, ("grp", "el"), ("az", "fq"), None)
    return jax.shard_map(
        pick, mesh=mesh, in_specs=in_specs, out_specs=out_specs, check_vma=False
    )
```

```python
import math

import jax
import jax.numpy as jnp
from jax import lax
from jax.experimental import pallas as pl
from jax.experimental.pallas import tpu as pltpu
from jax.sharding import PartitionSpec as P

F = 768
A = 1024
E = 32
HW = 8
KT = 8
LANES = 128
GROUP = 16
TAPS = 2 * HW + 1
BATCH = 4
LATE = 3
EARLY = 3
AHEAD = 10
HALVES = 2
SLOTS = 4
FIRST = 2
SPLIT = 2
TILE = 256
MESH = pl.DeviceIdType.MESH


def with_halo(cells, sides, width):
    for axis, dim in sides:
        count = lax.axis_size(axis)
        ends = count - 1
        head = lax.slice_in_dim(cells, 0, width, axis=dim)
        tail = lax.slice_in_dim(cells, cells.shape[dim] - width, cells.shape[dim], axis=dim)
        cells = jnp.concatenate(
            [
                lax.ppermute(tail, axis, [(i, (i + 1) % count) for i in range(ends)]),
                cells,
                lax.ppermute(head, axis, [((i + 1) % count, i) for i in range(ends)]),
            ],
            axis=dim,
        )
    return cells


def table_pair(row_ids, col_ids, length):
    product = row_ids[:, None] * col_ids[None, :] % length
    angle = product.astype(jnp.float32) * (2.0 * math.pi / length)
    return (jnp.cos(angle).astype(jnp.bfloat16), jnp.sin(angle).astype(jnp.bfloat16))


def on_device(polar, band_offset, tap_count, tap_weight):
    shape_all = polar.shape
    col_count = shape_all[2]
    freq_count = shape_all[3]
    az_count = lax.axis_size("az")
    fq_count = lax.axis_size("fq")
    el_count = lax.axis_size("el")
    padded = with_halo(polar, (("az", 2),), HW)
    window = col_count + 2 * HW
    column = jnp.arange(col_count, dtype=jnp.int32)[:, None]
    position = jnp.arange(window, dtype=jnp.int32)[None, :, None]
    band_matrix = jnp.zeros((col_count, window, freq_count), jnp.bfloat16)
    for tap_index in range(KT):
        reach = column + HW + band_offset + tap_index
        matches = (position == reach[:, None, :]) & (tap_index < tap_count)[:, None, :]
        band_matrix = jnp.where(matches, tap_weight[tap_index][:, None, :], band_matrix)
    interpolated = jnp.einsum(
        "jaf,ceaf->cejf", band_matrix, padded, preferred_element_type=jnp.float32
    ).astype(jnp.bfloat16)
    fq_index = lax.axis_index("fq")
    bin_count = F // (fq_count * az_count)
    az_block = jnp.arange(az_count, dtype=jnp.int32)[:, None]
    bin_local = jnp.arange(bin_count, dtype=jnp.int32)[None, :]
    range_bins = ((az_block * fq_count + fq_index) * bin_count + bin_local).reshape(-1)
    cos_f, sin_f = table_pair(jnp.arange(F, dtype=jnp.int32), range_bins, F)
    shard_piece = lax.all_gather(interpolated, "fq", axis=3, tiled=True)
    cos_rows = cos_f
    sin_rows = sin_f
    real_part = jnp.einsum(
        "ejf,fk->ekj", shard_piece[0], cos_rows, preferred_element_type=jnp.float32
    ) - jnp.einsum("ejf,fk->ekj", shard_piece[1], sin_rows, preferred_element_type=jnp.float32)
    imag_part = jnp.einsum(
        "ejf,fk->ekj", shard_piece[0], sin_rows, preferred_element_type=jnp.float32
    ) + jnp.einsum("ejf,fk->ekj", shard_piece[1], cos_rows, preferred_element_type=jnp.float32)
    summed = jnp.stack([real_part, imag_part])
    ranged = (summed * (1.0 / math.sqrt(F))).astype(jnp.bfloat16)
    azim_ids = jnp.arange(A, dtype=jnp.int32)
    cos_a, sin_a = table_pair(azim_ids, azim_ids, A)
    block_data = lax.all_to_all(ranged, "az", split_axis=2, concat_axis=3, tiled=True)
    real_part = jnp.einsum(
        "ekj,jm->ekm", block_data[0], cos_a, preferred_element_type=jnp.float32
    ) - jnp.einsum("ekj,jm->ekm", block_data[1], sin_a, preferred_element_type=jnp.float32)
    imag_part = jnp.einsum(
        "ekj,jm->ekm", block_data[0], sin_a, preferred_element_type=jnp.float32
    ) + jnp.einsum("ekj,jm->ekm", block_data[1], cos_a, preferred_element_type=jnp.float32)
    crossed = (jnp.stack([real_part, imag_part]) * (1.0 / math.sqrt(A))).astype(jnp.bfloat16)
    elev_ids = jnp.arange(E, dtype=jnp.int32)
    el_index = lax.axis_index("el")
    height_count = E // el_count
    height_rows = el_index * height_count + jnp.arange(height_count, dtype=jnp.int32)
    cos_e, sin_e = table_pair(elev_ids, height_rows, E)
    shard_piece = lax.all_gather(crossed, "el", axis=1, tiled=True)
    cos_rows = cos_e
    sin_rows = sin_e
    real_part = jnp.einsum(
        "eh,ekm->hkm", cos_rows, shard_piece[0], preferred_element_type=jnp.float32
    ) - jnp.einsum("eh,ekm->hkm", sin_rows, shard_piece[1], preferred_element_type=jnp.float32)
    imag_part = jnp.einsum(
        "eh,ekm->hkm", sin_rows, shard_piece[0], preferred_element_type=jnp.float32
    ) + jnp.einsum("eh,ekm->hkm", cos_rows, shard_piece[1], preferred_element_type=jnp.float32)
    totals = jnp.stack([real_part, imag_part])
    image_out = (totals * (1.0 / math.sqrt(E))).astype(jnp.bfloat16)
    return image_out


def small_trig(product, length):
    value = product.astype(jnp.float32)
    turns = jnp.floor(value * (1.0 / length))
    angle = (value - turns * length) * (2.0 * math.pi / length)
    return jnp.cos(angle), jnp.sin(angle)


def iota(shape, dim):
    return lax.broadcasted_iota(jnp.int32, shape, dim)


def fused_body(
    polar, off_h, cnt_h, tap_h, out_h,
    xs, buf, pv, wt, offv, cntv, tapv, hl, hr,
    lowc, lows, highc, highs, rtab, cos_a, sin_a, htab,
    rl, zl, er, eh, ez, ch, ost, est,
    in_sem, pv_sem, halo_s, halo_r, fq_s, fq_r, zl_s, zl_r,
    xe_s, xe_r, ze_s, ze_r, xa_s, xa_r, xb_s, xb_r, lo_sem, eo_sem,
):
    n_az = lax.axis_size("az")
    az, fq, el = (lax.axis_index(name) for name in ("az", "fq", "el"))
    _, cuts, cols, freqs = polar.shape
    parts = freqs // LANES
    heights = E // 2
    late = LATE * GROUP
    bins = out_h.shape[2]
    early_groups = (bins - late) // GROUP
    batches = cuts // BATCH
    steps = cols // GROUP

    def at_az(shift):
        return {"az": lax.rem(az + shift, n_az)}

    def lane_block(index, size):
        return pl.ds(pl.multiple_of(index * size, LANES), size)

    fq_peer = {"fq": 1 - fq}
    el_peer = {"el": 1 - el}
    own_cols = lane_block(az, cols)

    def from_az(shift):
        return lane_block(lax.rem(az - shift + n_az, n_az), cols)

    def remote(source, target, send, recv, where):
        return pltpu.make_async_remote_copy(
            src_ref=source,
            dst_ref=target,
            send_sem=send,
            recv_sem=recv,
            device_id=where,
            device_id_type=MESH,
        )

    def polar_copy(c):
        slot = lax.rem(c, SLOTS)
        return pltpu.make_async_copy(polar.at[:, c], pv.at[slot], pv_sem.at[slot])

    spans = (pl.ds(0, FIRST), pl.ds(FIRST, cuts - FIRST))

    def halo_up(k):
        return remote(
            polar.at[:, spans[k], pl.ds(cols - HW, HW)],
            hl.at[:, spans[k]],
            halo_s.at[0, k],
            halo_r.at[0, k],
            at_az(1),
        )

    def halo_down(k):
        return remote(
            polar.at[:, spans[k], pl.ds(0, HW)],
            hr.at[:, spans[k]],
            halo_s.at[1, k],
            halo_r.at[1, k],
            at_az(n_az - 1),
        )

    def fq_copy(c, lanes):
        return remote(
            xs.at[c, :, :, lanes], xs.at[c, :, :, lanes], fq_s.at[c], fq_r.at[c], fq_peer
        )

    def zl_copy(c, shift, lanes):
        return remote(
            rl.at[c, shift - 1],
            zl.at[c // BATCH, :, lax.rem(c, BATCH), :, lanes],
            zl_s.at[c, shift - 1],
            zl_r.at[c, shift - 1],
            at_az(shift),
        )

    def xe_copy(c, g):
        return remote(
            er.at[g, :, 0, :, c],
            er.at[g, :, 1, :, c],
            xe_s.at[c, g],
            xe_r.at[c, g],
            el_peer,
        )

    def ze_copy(g, q, shift, lanes):
        span = pl.ds(q * (heights // SPLIT), heights // SPLIT)
        return remote(
            eh.at[g, shift - 1, :, span],
            ez.at[g, :, span, :, lanes],
            ze_s.at[g, q, shift - 1],
            ze_r.at[g, q, shift - 1],
            at_az(shift),
        )

    def xa_copy(b):
        span = pl.ds(b * BATCH, BATCH)
        return remote(
            ch.at[:, 0, :, span], ch.at[:, 1, :, span], xa_s.at[b], xa_r.at[b], el_peer
        )

    def xb_copy(b, g, k):
        span = pl.ds(b * BATCH, BATCH)
        half = batches // 2
        lanes = pl.ds(k * (A // HALVES), A // HALVES)
        return remote(
            ch.at[g, 0, :, span, :, lanes],
            ch.at[g, 1, :, span, :, lanes],
            xb_s.at[b - half, g, k],
            xb_r.at[b - half, g, k],
            el_peer,
        )

    barrier = pltpu.get_barrier_semaphore()
    peers = [fq_peer, el_peer] + [at_az(s) for s in range(1, n_az)]
    for peer in peers:
        pl.semaphore_signal(barrier, inc=1, device_id=peer, device_id_type=MESH)
    loads = [
        pltpu.make_async_copy(off_h, offv, in_sem.at[0]),
        pltpu.make_async_copy(cnt_h, cntv, in_sem.at[1]),
        pltpu.make_async_copy(tap_h, tapv, in_sem.at[2]),
    ]
    for load in loads:
        load.start()
    for c in range(SLOTS):
        polar_copy(c).start()

    @pl.when(az == 0)
    def _():
        hl[...] = jnp.zeros(hl.shape, hl.dtype)

    @pl.when(az == n_az - 1)
    def _():
        hr[...] = jnp.zeros(hr.shape, hr.dtype)

    pl.semaphore_wait(barrier, len(peers))

    @pl.when(az < n_az - 1)
    def _():
        for k in range(2):
            halo_up(k).start()

    @pl.when(az > 0)
    def _():
        for k in range(2):
            halo_down(k).start()

    block = 32
    blocks = n_az * bins // block
    per = bins // block
    row = iota((16, F), 0)
    shift = jnp.zeros((16, F), jnp.int32)
    for s in range(1, n_az):
        shift = shift + (row >= s * per).astype(jnp.int32)
    inner = row - shift * per
    target = az + shift
    target = jnp.where(target >= n_az, target - n_az, target)
    starts = (target * 2 + fq) * bins + inner * block
    wide = slice(0, F)
    highc[0:16, wide], highs[0:16, wide] = small_trig(starts * iota((16, F), 1), F)
    lowc[:, wide], lows[:, wide] = small_trig(iota((block, F), 0) * iota((block, F), 1), F)

    @pl.loop(0, blocks)
    def _(i):
        hc, hs = highc[pl.ds(i, 1), wide], highs[pl.ds(i, 1), wide]
        lc, ls = lowc[:, wide], lows[:, wide]
        at = pl.ds(pl.multiple_of(i * block, block), block)
        rtab[at, :] = (hc * lc - hs * ls).astype(jnp.bfloat16)
        at = pl.ds(pl.multiple_of((blocks + i) * block, block), block)
        rtab[at, :] = (hs * lc + hc * ls).astype(jnp.bfloat16)

    for load in loads:
        load.wait()

    @pl.loop(0, parts * steps)
    def _(i):
        g = i // steps
        rows = pl.ds(pl.multiple_of(lax.rem(i, steps) * GROUP, GROUP), GROUP)
        lanes = lane_block(g, LANES)
        rel = offv[rows, lanes] + HW
        cnt = cntv[rows, lanes]
        zero = jnp.zeros(rel.shape, jnp.float32)
        taps = [
            jnp.where(t < cnt, tapv[t, rows, lanes].astype(jnp.float32), zero)
            for t in range(KT)
        ]
        for bit in range(4):
            step = 1 << bit
            on = (rel & step) != 0
            size = min(TAPS, len(taps) + step)
            taps = [
                jnp.where(
                    on,
                    taps[d - step] if d >= step else zero,
                    taps[d] if d < len(taps) else zero,
                )
                for d in range(size)
            ]
        for d in range(TAPS):
            wt[d, g, rows, :] = taps[d]

    def wait_halo(k):
        @pl.when(az > 0)
        def _():
            halo_up(k).wait_recv()

        @pl.when(az < n_az - 1)
        def _():
            halo_down(k).wait_recv()

    def interpolate(c):
        slot = lax.rem(c, SLOTS)
        polar_copy(c).wait()

        @pl.when(c == 0)
        def _():
            wait_halo(0)

        @pl.when(c == FIRST)
        def _():
            wait_halo(1)

        for p in range(2):
            for g in range(parts):
                lanes = slice(g * LANES, (g + 1) * LANES)
                buf[p, g, 0:HW, :] = hl[p, c, :, lanes].astype(jnp.float32)
                buf[p, g, HW : HW + cols, :] = pv[slot, p, :, lanes].astype(jnp.float32)
                buf[p, g, HW + cols :, :] = hr[p, c, :, lanes].astype(jnp.float32)

        @pl.loop(0, parts * steps)
        def _(i):
            g = i // steps
            base = pl.multiple_of(lax.rem(i, steps) * GROUP, GROUP)
            lanes = lane_block(fq * parts + g, LANES)
            weights = [wt[d, g, pl.ds(base, GROUP), :] for d in range(TAPS)]
            for p in range(2):
                acc = [None, None]
                for o in range(TAPS + 8):
                    cell = buf[p, g, pl.ds(base + o, 8), :]
                    for v in range(2):
                        d = o - 8 * v
                        if 0 <= d < TAPS:
                            term = weights[d][8 * v : 8 * v + 8] * cell
                            acc[v] = term if acc[v] is None else acc[v] + term
                value = jnp.concatenate(acc, axis=0).astype(jnp.bfloat16)
                xs[c, p, pl.ds(base, GROUP), lanes] = value

        fq_copy(c, lane_block(fq, freqs)).start()

        @pl.when(c + SLOTS < cuts)
        def _():
            polar_copy(c + SLOTS).start()

    def range_step(c):
        fq_copy(c, lane_block(1 - fq, freqs)).wait_recv()
        dims = (((1,), (1,)), ((), ()))
        table = rtab[...]
        fr = lax.dot_general(table, xs[c, 0], dims, preferred_element_type=jnp.float32)
        fi = lax.dot_general(table, xs[c, 1], dims, preferred_element_type=jnp.float32)
        half = n_az * bins
        scale = 1.0 / math.sqrt(F)
        real = ((fr[:half] - fi[half:]) * scale).astype(jnp.bfloat16)
        imag = ((fr[half:] + fi[:half]) * scale).astype(jnp.bfloat16)
        b, k = c // BATCH, lax.rem(c, BATCH)
        for p, part in enumerate((real, imag)):
            for s in range(n_az):
                piece = part[s * bins : s * bins + late]
                if s == 0:
                    zl[b, p, k, :, own_cols] = piece
                else:
                    rl[c, s - 1, p] = piece
                for g in range(early_groups):
                    at = s * bins + late + g * GROUP
                    er[g, s, 0, p, c] = part[at : at + GROUP]
        for core, shifts in enumerate((order[1:] + order[:1], order)):

            @pl.when(fq == core)
            def _():
                for s in shifts:
                    zl_copy(c, s, own_cols).start()

        for g in range(early_groups - 1):
            xe_copy(c, g).start()

        @pl.when(c < AHEAD)
        def _():
            xe_copy(c, early_groups - 1).start()

    order = list(range(1, n_az))

    def azimuth_tables():
        col = iota((block, A), 1)
        lowc[...], lows[...] = small_trig(iota((block, A), 0) * col, A)
        highc[...], highs[...] = small_trig(iota((A // block, A), 0) * block * col, A)

        @pl.loop(0, A // block)
        def _(i):
            hc, hs = highc[pl.ds(i, 1), :], highs[pl.ds(i, 1), :]
            at = pl.ds(pl.multiple_of(i * block, block), block)
            cos_a[at, :] = (hc * lowc[...] - hs * lows[...]).astype(jnp.bfloat16)
            sin_a[at, :] = (hs * lowc[...] + hc * lows[...]).astype(jnp.bfloat16)

    def height_tables():
        rows, width = 2 * heights, 4 * cuts
        row, col = iota((rows, 128), 0), iota((rows, 128), 1)
        out_imag = row >= heights
        height = el * heights + jnp.where(out_imag, row - heights, row)
        other = col >= 2 * cuts
        inner = jnp.where(other, col - 2 * cuts, col)
        in_imag = inner >= cuts
        source = jnp.where(other, 1 - el, el)
        elev = source * cuts + jnp.where(in_imag, inner - cuts, inner)
        cos_e, sin_e = small_trig(height * elev, E)
        sign = jnp.where(out_imag, sin_e, -sin_e)
        small = jnp.where(out_imag == in_imag, cos_e, sign)
        small = jnp.where(col < width, small, 0.0).astype(jnp.bfloat16)
        tall = rows * GROUP
        take_row = (iota((tall, rows), 0) // GROUP == iota((tall, rows), 1)).astype(
            jnp.bfloat16
        )
        mid = jnp.dot(take_row, small, preferred_element_type=jnp.float32)
        mid = mid.astype(jnp.bfloat16)

        @pl.loop(0, width * GROUP // TILE)
        def _(i):
            shape = (128, TILE)
            col_at = iota(shape, 1) + i * TILE
            take_col = (iota(shape, 0) == col_at // GROUP).astype(jnp.bfloat16)
            spread = jnp.dot(mid, take_col, preferred_element_type=jnp.float32)
            shape = (tall, TILE)
            same = (iota(shape, 0) & (GROUP - 1)) == (iota(shape, 1) & (GROUP - 1))
            htab[:, lane_block(i, TILE)] = jnp.where(same, spread, 0.0).astype(jnp.bfloat16)

    def cross_tile(left, t):
        rows = left.shape[0] // 2
        scale = 1.0 / math.sqrt(A)
        by_cos = jnp.dot(left, cos_a[:, lane_block(t, TILE)], preferred_element_type=jnp.float32)
        by_sin = jnp.dot(left, sin_a[:, lane_block(t, TILE)], preferred_element_type=jnp.float32)
        real = ((by_cos[:rows] - by_sin[rows:]) * scale).astype(jnp.bfloat16)
        imag = ((by_sin[:rows] + by_cos[rows:]) * scale).astype(jnp.bfloat16)
        return real, imag

    def cross_late(b):
        for k in range(BATCH):
            for s in order:
                zl_copy(b * BATCH + k, s, from_az(s)).wait_recv()

        @pl.loop(0, A // TILE)
        def _(t):
            left = zl[b].reshape(2 * BATCH * late, A)
            for p, part in enumerate(cross_tile(left, t)):
                part = part.reshape(BATCH, LATE, GROUP, TILE)
                for g in range(LATE):
                    span = pl.ds(b * BATCH, BATCH)
                    ch[g, 0, p, span, :, lane_block(t, TILE)] = part[:, g]

    def early_heights(g):
        for c in range(cuts):
            xe_copy(c, g).wait_recv()

        @pl.loop(0, n_az)
        def _(s):
            data = er[g, s].reshape(4 * cuts * GROUP, cols)
            total = jnp.dot(htab[...], data, preferred_element_type=jnp.float32)
            total = (total * (1.0 / math.sqrt(E))).astype(jnp.bfloat16)
            total = total.reshape(2, heights, GROUP, cols)

            @pl.when(s == 0)
            def _():
                ez[g, :, :, :, own_cols] = total

            @pl.when(s > 0)
            def _():
                eh[g, s - 1] = total

        for q in range(SPLIT):
            for s in order:
                ze_copy(g, q, s, own_cols).start()

    def early_out(g, q):
        span = pl.ds(q * (heights // SPLIT), heights // SPLIT)
        return pltpu.make_async_copy(
            est.at[g, q],
            out_h.at[:, span, pl.ds(late + g * GROUP, GROUP), :],
            eo_sem.at[g, q],
        )

    def cross_early(g, q):
        for s in order:
            ze_copy(g, q, s, from_az(s)).wait_recv()
        some = heights // SPLIT

        @pl.loop(0, A // TILE)
        def _(t):
            left = ez[g, :, q * some : (q + 1) * some].reshape(2 * some * GROUP, A)
            for p, part in enumerate(cross_tile(left, t)):
                est[g, q, p, :, :, lane_block(t, TILE)] = part.reshape(some, GROUP, TILE)

        early_out(g, q).start()

    def late_out(g):
        return pltpu.make_async_copy(
            ost.at[g % 2], out_h.at[:, :, pl.ds(g * GROUP, GROUP), :], lo_sem.at[g]
        )

    def late_heights(g, k):
        if g == 0 and k == 0:
            for b in range(batches // 2):
                xa_copy(b).wait_recv()
        for b in range(batches // 2, batches):
            xb_copy(b, g, k).wait_recv()
        if g >= 2 and k == 0:
            late_out(g - 2).wait()
        some = A // TILE // HALVES

        @pl.loop(k * some, (k + 1) * some)
        def _(t):
            at = lane_block(t, TILE)
            data = ch[g, :, :, :, :, at].reshape(4 * cuts * GROUP, TILE)
            total = jnp.dot(htab[...], data, preferred_element_type=jnp.float32)
            total = (total * (1.0 / math.sqrt(E))).astype(jnp.bfloat16)
            ost[g % 2, :, :, :, at] = total.reshape(2, heights, GROUP, TILE)

        if k == HALVES - 1:
            late_out(g).start()

    def front(first, last):
        @pl.loop(first, last)
        def _(c):
            @pl.when(c < cuts)
            def _():
                interpolate(c)

            @pl.when(c > 0)
            def _():
                range_step(c - 1)

    front(0, cuts + 1)
    for c in range(AHEAD, cuts):
        xe_copy(c, early_groups - 1).start()
    height_tables()
    early_heights(0)
    azimuth_tables()
    cross_late(0)
    xa_copy(0).start()
    cross_late(1)
    xa_copy(1).start()
    for g in range(1, early_groups):
        early_heights(g)
    for b in range(batches // 2, batches):
        cross_late(b)
    for g in range(LATE):
        for k in range(HALVES):
            for b in range(batches // 2, batches):
                xb_copy(b, g, k).start()
    cross_early(0, 0)
    cross_early(0, 1)
    cross_early(1, 0)
    late_heights(0, 0)
    late_heights(0, 1)
    cross_early(1, 1)
    late_heights(1, 0)
    late_heights(1, 1)
    cross_early(2, 0)
    late_heights(2, 0)
    cross_early(2, 1)
    late_heights(2, 1)

    @pl.when(az < n_az - 1)
    def _():
        for k in range(2):
            halo_up(k).wait_send()

    @pl.when(az > 0)
    def _():
        for k in range(2):
            halo_down(k).wait_send()

    @pl.loop(0, cuts)
    def _(c):
        fq_copy(c, lane_block(fq, freqs)).wait_send()
        for s in order:
            zl_copy(c, s, own_cols).wait_send()
        for g in range(early_groups):
            xe_copy(c, g).wait_send()

    for g in range(early_groups):
        for q in range(SPLIT):
            for s in order:
                ze_copy(g, q, s, own_cols).wait_send()
    for b in range(batches // 2):
        xa_copy(b).wait_send()
    for b in range(batches // 2, batches):
        for g in range(LATE):
            for k in range(HALVES):
                xb_copy(b, g, k).wait_send()
    for g in range(early_groups):
        for q in range(SPLIT):
            early_out(g, q).wait()
    for g in range(LATE - 2, LATE):
        late_out(g).wait()


def fused(polar, band_offset, tap_count, tap_weight):
    _, cuts, cols, freqs = polar.shape
    n_az = lax.axis_size("az")
    bins = F // (2 * n_az)
    late = LATE * GROUP
    heights = E // 2
    parts = freqs // LANES
    groups = (bins - late) // GROUP
    batches = cuts // BATCH
    far = n_az - 1
    half = jnp.bfloat16
    vmem = pltpu.VMEM
    dma = pltpu.SemaphoreType.DMA
    return pl.pallas_call(
        fused_body,
        out_shape=jax.ShapeDtypeStruct((2, heights, bins, A), half),
        in_specs=[pl.BlockSpec(memory_space=pl.ANY)] * 4,
        out_specs=pl.BlockSpec(memory_space=pl.ANY),
        scratch_shapes=[
            vmem((cuts, 2, cols, F), half),
            vmem((2, parts, cols + 2 * HW, LANES), jnp.float32),
            vmem((SLOTS, 2, cols, freqs), half),
            vmem((TAPS, parts, cols, LANES), jnp.float32),
            vmem((cols, freqs), jnp.int32),
            vmem((cols, freqs), jnp.int32),
            vmem((KT, cols, freqs), half),
            vmem((2, cuts, HW, freqs), half),
            vmem((2, cuts, HW, freqs), half),
            vmem((32, A), jnp.float32),
            vmem((32, A), jnp.float32),
            vmem((32, A), jnp.float32),
            vmem((32, A), jnp.float32),
            vmem((2 * n_az * bins, F), half),
            vmem((A, A), half),
            vmem((A, A), half),
            vmem((2 * heights * GROUP, 4 * cuts * GROUP), half),
            vmem((cuts, far, 2, late, cols), half),
            vmem((batches, 2, BATCH, late, A), half),
            vmem((groups, n_az, 2, 2, cuts, GROUP, cols), half),
            vmem((groups, far, 2, heights, GROUP, cols), half),
            vmem((groups, 2, heights, GROUP, A), half),
            vmem((LATE, 2, 2, cuts, GROUP, A), half),
            vmem((2, 2, heights, GROUP, A), half),
            vmem((groups, SPLIT, 2, heights // SPLIT, GROUP, A), half),
            dma((3,)),
            dma((SLOTS,)),
            dma((2, 2)),
            dma((2, 2)),
            dma((cuts,)),
            dma((cuts,)),
            dma((cuts, far)),
            dma((cuts, far)),
            dma((cuts, groups)),
            dma((cuts, groups)),
            dma((groups, SPLIT, far)),
            dma((groups, SPLIT, far)),
            dma((batches // 2,)),
            dma((batches // 2,)),
            dma((batches // 2, LATE, HALVES)),
            dma((batches // 2, LATE, HALVES)),
            dma((LATE,)),
            dma((groups, SPLIT)),
        ],
        compiler_params=pltpu.CompilerParams(
            collective_id=0, has_side_effects=True, vmem_limit_bytes=67043328
        ),
        name="image",
    )(polar, band_offset, tap_count, tap_weight)


def pick(polar, band_offset, tap_count, tap_weight):
    _, e_here, col_count, freq_count = polar.shape
    az_count = lax.axis_size("az")
    bins = F // (lax.axis_size("fq") * az_count)
    fits = (
        lax.axis_size("fq") == 2
        and lax.axis_size("el") == 2
        and az_count == 4
        and e_here == 4 * BATCH
        and bins == (LATE + EARLY) * GROUP
        and col_count == TILE
        and freq_count % LANES == 0
    )
    run = fused if fits else on_device
    return run(polar, band_offset, tap_count, tap_weight)


def solution(mesh):
    in_specs = (
        P(None, ("grp", "el"), "az", "fq"),
        P("az", "fq"),
        P("az", "fq"),
        P(None, "az", "fq"),
    )
    out_specs = P(None, ("grp", "el"), ("az", "fq"), None)
    return jax.shard_map(
        pick, mesh=mesh, in_specs=in_specs, out_specs=out_specs, check_vma=False
    )
```

```python
import math

import jax
import jax.numpy as jnp
from jax import lax
from jax.experimental import pallas as pl
from jax.experimental.pallas import tpu as pltpu
from jax.sharding import PartitionSpec as P

F = 768
A = 1024
E = 32
HW = 8
KT = 8
LANES = 128
GROUP = 16
TAPS = 2 * HW + 1
BATCH = 4
LATE = 3
EARLY = 3
AHEAD = 10
HALVES = 2
SLOTS = 4
FIRST = 2
SPLIT = 2
TILE = 256
MESH = pl.DeviceIdType.MESH


def with_halo(cells, sides, width):
    for axis, dim in sides:
        count = lax.axis_size(axis)
        ends = count - 1
        head = lax.slice_in_dim(cells, 0, width, axis=dim)
        tail = lax.slice_in_dim(cells, cells.shape[dim] - width, cells.shape[dim], axis=dim)
        cells = jnp.concatenate(
            [
                lax.ppermute(tail, axis, [(i, (i + 1) % count) for i in range(ends)]),
                cells,
                lax.ppermute(head, axis, [((i + 1) % count, i) for i in range(ends)]),
            ],
            axis=dim,
        )
    return cells


def table_pair(row_ids, col_ids, length):
    product = row_ids[:, None] * col_ids[None, :] % length
    angle = product.astype(jnp.float32) * (2.0 * math.pi / length)
    return (jnp.cos(angle).astype(jnp.bfloat16), jnp.sin(angle).astype(jnp.bfloat16))


def on_device(polar, band_offset, tap_count, tap_weight):
    shape_all = polar.shape
    col_count = shape_all[2]
    freq_count = shape_all[3]
    az_count = lax.axis_size("az")
    fq_count = lax.axis_size("fq")
    el_count = lax.axis_size("el")
    padded = with_halo(polar, (("az", 2),), HW)
    window = col_count + 2 * HW
    column = jnp.arange(col_count, dtype=jnp.int32)[:, None]
    position = jnp.arange(window, dtype=jnp.int32)[None, :, None]
    band_matrix = jnp.zeros((col_count, window, freq_count), jnp.bfloat16)
    for tap_index in range(KT):
        reach = column + HW + band_offset + tap_index
        matches = (position == reach[:, None, :]) & (tap_index < tap_count)[:, None, :]
        band_matrix = jnp.where(matches, tap_weight[tap_index][:, None, :], band_matrix)
    interpolated = jnp.einsum(
        "jaf,ceaf->cejf", band_matrix, padded, preferred_element_type=jnp.float32
    ).astype(jnp.bfloat16)
    fq_index = lax.axis_index("fq")
    bin_count = F // (fq_count * az_count)
    az_block = jnp.arange(az_count, dtype=jnp.int32)[:, None]
    bin_local = jnp.arange(bin_count, dtype=jnp.int32)[None, :]
    range_bins = ((az_block * fq_count + fq_index) * bin_count + bin_local).reshape(-1)
    cos_f, sin_f = table_pair(jnp.arange(F, dtype=jnp.int32), range_bins, F)
    shard_piece = lax.all_gather(interpolated, "fq", axis=3, tiled=True)
    cos_rows = cos_f
    sin_rows = sin_f
    real_part = jnp.einsum(
        "ejf,fk->ekj", shard_piece[0], cos_rows, preferred_element_type=jnp.float32
    ) - jnp.einsum("ejf,fk->ekj", shard_piece[1], sin_rows, preferred_element_type=jnp.float32)
    imag_part = jnp.einsum(
        "ejf,fk->ekj", shard_piece[0], sin_rows, preferred_element_type=jnp.float32
    ) + jnp.einsum("ejf,fk->ekj", shard_piece[1], cos_rows, preferred_element_type=jnp.float32)
    summed = jnp.stack([real_part, imag_part])
    ranged = (summed * (1.0 / math.sqrt(F))).astype(jnp.bfloat16)
    azim_ids = jnp.arange(A, dtype=jnp.int32)
    cos_a, sin_a = table_pair(azim_ids, azim_ids, A)
    block_data = lax.all_to_all(ranged, "az", split_axis=2, concat_axis=3, tiled=True)
    real_part = jnp.einsum(
        "ekj,jm->ekm", block_data[0], cos_a, preferred_element_type=jnp.float32
    ) - jnp.einsum("ekj,jm->ekm", block_data[1], sin_a, preferred_element_type=jnp.float32)
    imag_part = jnp.einsum(
        "ekj,jm->ekm", block_data[0], sin_a, preferred_element_type=jnp.float32
    ) + jnp.einsum("ekj,jm->ekm", block_data[1], cos_a, preferred_element_type=jnp.float32)
    crossed = (jnp.stack([real_part, imag_part]) * (1.0 / math.sqrt(A))).astype(jnp.bfloat16)
    elev_ids = jnp.arange(E, dtype=jnp.int32)
    el_index = lax.axis_index("el")
    height_count = E // el_count
    height_rows = el_index * height_count + jnp.arange(height_count, dtype=jnp.int32)
    cos_e, sin_e = table_pair(elev_ids, height_rows, E)
    shard_piece = lax.all_gather(crossed, "el", axis=1, tiled=True)
    cos_rows = cos_e
    sin_rows = sin_e
    real_part = jnp.einsum(
        "eh,ekm->hkm", cos_rows, shard_piece[0], preferred_element_type=jnp.float32
    ) - jnp.einsum("eh,ekm->hkm", sin_rows, shard_piece[1], preferred_element_type=jnp.float32)
    imag_part = jnp.einsum(
        "eh,ekm->hkm", sin_rows, shard_piece[0], preferred_element_type=jnp.float32
    ) + jnp.einsum("eh,ekm->hkm", cos_rows, shard_piece[1], preferred_element_type=jnp.float32)
    totals = jnp.stack([real_part, imag_part])
    image_out = (totals * (1.0 / math.sqrt(E))).astype(jnp.bfloat16)
    return image_out


def small_trig(product, length):
    value = product.astype(jnp.float32)
    turns = jnp.floor(value * (1.0 / length))
    angle = (value - turns * length) * (2.0 * math.pi / length)
    return jnp.cos(angle), jnp.sin(angle)


def iota(shape, dim):
    return lax.broadcasted_iota(jnp.int32, shape, dim)


def fused_body(
    polar, off_h, cnt_h, tap_h, out,
    xs, buf, pv, wt, offv, cntv, tapv, hl, hr,
    lowc, lows, highc, highs, rtab, cos_a, sin_a, htab,
    rl, zl, er, eh, ez, ch,
    in_sem, pv_sem, halo_s, halo_r, fq_s, fq_r, zl_s, zl_r,
    xe_s, xe_r, ze_s, ze_r, xa_s, xa_r, xb_s, xb_r,
):
    n_az = lax.axis_size("az")
    az, fq, el = (lax.axis_index(name) for name in ("az", "fq", "el"))
    _, cuts, cols, freqs = polar.shape
    parts = freqs // LANES
    heights = E // 2
    late = LATE * GROUP
    bins = out.shape[2]
    early_groups = (bins - late) // GROUP
    batches = cuts // BATCH
    steps = cols // GROUP

    def at_az(shift):
        return {"az": lax.rem(az + shift, n_az)}

    def lane_block(index, size):
        return pl.ds(pl.multiple_of(index * size, LANES), size)

    fq_peer = {"fq": 1 - fq}
    el_peer = {"el": 1 - el}
    own_cols = lane_block(az, cols)

    def from_az(shift):
        return lane_block(lax.rem(az - shift + n_az, n_az), cols)

    def remote(source, target, send, recv, where):
        return pltpu.make_async_remote_copy(
            src_ref=source,
            dst_ref=target,
            send_sem=send,
            recv_sem=recv,
            device_id=where,
            device_id_type=MESH,
        )

    def polar_copy(c):
        slot = lax.rem(c, SLOTS)
        return pltpu.make_async_copy(polar.at[:, c], pv.at[slot], pv_sem.at[slot])

    spans = (pl.ds(0, FIRST), pl.ds(FIRST, cuts - FIRST))

    def halo_up(k):
        return remote(
            polar.at[:, spans[k], pl.ds(cols - HW, HW)],
            hl.at[:, spans[k]],
            halo_s.at[0, k],
            halo_r.at[0, k],
            at_az(1),
        )

    def halo_down(k):
        return remote(
            polar.at[:, spans[k], pl.ds(0, HW)],
            hr.at[:, spans[k]],
            halo_s.at[1, k],
            halo_r.at[1, k],
            at_az(n_az - 1),
        )

    def fq_copy(c, lanes):
        return remote(
            xs.at[c, :, :, lanes], xs.at[c, :, :, lanes], fq_s.at[c], fq_r.at[c], fq_peer
        )

    def zl_copy(c, shift, lanes):
        return remote(
            rl.at[c, shift - 1],
            zl.at[c // BATCH, :, lax.rem(c, BATCH), :, lanes],
            zl_s.at[c, shift - 1],
            zl_r.at[c, shift - 1],
            at_az(shift),
        )

    def xe_copy(c, g):
        return remote(
            er.at[g, :, 0, :, c],
            er.at[g, :, 1, :, c],
            xe_s.at[c, g],
            xe_r.at[c, g],
            el_peer,
        )

    def ze_copy(g, q, shift, lanes):
        span = pl.ds(q * (heights // SPLIT), heights // SPLIT)
        return remote(
            eh.at[g, shift - 1, :, span],
            ez.at[g, :, span, :, lanes],
            ze_s.at[g, q, shift - 1],
            ze_r.at[g, q, shift - 1],
            at_az(shift),
        )

    def xa_copy(b):
        span = pl.ds(b * BATCH, BATCH)
        return remote(
            ch.at[:, 0, :, span], ch.at[:, 1, :, span], xa_s.at[b], xa_r.at[b], el_peer
        )

    def xb_copy(b, g, k):
        span = pl.ds(b * BATCH, BATCH)
        half = batches // 2
        lanes = pl.ds(k * (A // HALVES), A // HALVES)
        return remote(
            ch.at[g, 0, :, span, :, lanes],
            ch.at[g, 1, :, span, :, lanes],
            xb_s.at[b - half, g, k],
            xb_r.at[b - half, g, k],
            el_peer,
        )

    barrier = pltpu.get_barrier_semaphore()
    peers = [fq_peer, el_peer] + [at_az(s) for s in range(1, n_az)]
    for peer in peers:
        pl.semaphore_signal(barrier, inc=1, device_id=peer, device_id_type=MESH)
    loads = [
        pltpu.make_async_copy(off_h, offv, in_sem.at[0]),
        pltpu.make_async_copy(cnt_h, cntv, in_sem.at[1]),
        pltpu.make_async_copy(tap_h, tapv, in_sem.at[2]),
    ]
    for load in loads:
        load.start()
    for c in range(SLOTS):
        polar_copy(c).start()

    @pl.when(az == 0)
    def _():
        hl[...] = jnp.zeros(hl.shape, hl.dtype)

    @pl.when(az == n_az - 1)
    def _():
        hr[...] = jnp.zeros(hr.shape, hr.dtype)

    pl.semaphore_wait(barrier, len(peers))

    @pl.when(az < n_az - 1)
    def _():
        for k in range(2):
            halo_up(k).start()

    @pl.when(az > 0)
    def _():
        for k in range(2):
            halo_down(k).start()

    block = 32
    blocks = n_az * bins // block
    per = bins // block
    row = iota((16, F), 0)
    shift = jnp.zeros((16, F), jnp.int32)
    for s in range(1, n_az):
        shift = shift + (row >= s * per).astype(jnp.int32)
    inner = row - shift * per
    target = az + shift
    target = jnp.where(target >= n_az, target - n_az, target)
    starts = (target * 2 + fq) * bins + inner * block
    wide = slice(0, F)
    highc[0:16, wide], highs[0:16, wide] = small_trig(starts * iota((16, F), 1), F)
    lowc[:, wide], lows[:, wide] = small_trig(iota((block, F), 0) * iota((block, F), 1), F)

    @pl.loop(0, blocks)
    def _(i):
        hc, hs = highc[pl.ds(i, 1), wide], highs[pl.ds(i, 1), wide]
        lc, ls = lowc[:, wide], lows[:, wide]
        at = pl.ds(pl.multiple_of(i * block, block), block)
        rtab[at, :] = (hc * lc - hs * ls).astype(jnp.bfloat16)
        at = pl.ds(pl.multiple_of((blocks + i) * block, block), block)
        rtab[at, :] = (hs * lc + hc * ls).astype(jnp.bfloat16)

    for load in loads:
        load.wait()

    @pl.loop(0, parts * steps)
    def _(i):
        g = i // steps
        rows = pl.ds(pl.multiple_of(lax.rem(i, steps) * GROUP, GROUP), GROUP)
        lanes = lane_block(g, LANES)
        rel = offv[rows, lanes] + HW
        cnt = cntv[rows, lanes]
        zero = jnp.zeros(rel.shape, jnp.float32)
        taps = [
            jnp.where(t < cnt, tapv[t, rows, lanes].astype(jnp.float32), zero)
            for t in range(KT)
        ]
        for bit in range(4):
            step = 1 << bit
            on = (rel & step) != 0
            size = min(TAPS, len(taps) + step)
            taps = [
                jnp.where(
                    on,
                    taps[d - step] if d >= step else zero,
                    taps[d] if d < len(taps) else zero,
                )
                for d in range(size)
            ]
        for d in range(TAPS):
            wt[d, g, rows, :] = taps[d].astype(jnp.bfloat16)

    def wait_halo(k):
        @pl.when(az > 0)
        def _():
            halo_up(k).wait_recv()

        @pl.when(az < n_az - 1)
        def _():
            halo_down(k).wait_recv()

    def interpolate(c):
        slot = lax.rem(c, SLOTS)
        polar_copy(c).wait()

        @pl.when(c == 0)
        def _():
            wait_halo(0)

        @pl.when(c == FIRST)
        def _():
            wait_halo(1)

        for p in range(2):
            for g in range(parts):
                lanes = slice(g * LANES, (g + 1) * LANES)
                buf[p, g, 0:HW, :] = hl[p, c, :, lanes].astype(jnp.float32)
                buf[p, g, HW : HW + cols, :] = pv[slot, p, :, lanes].astype(jnp.float32)
                buf[p, g, HW + cols :, :] = hr[p, c, :, lanes].astype(jnp.float32)

        @pl.loop(0, parts * steps)
        def _(i):
            g = i // steps
            base = pl.multiple_of(lax.rem(i, steps) * GROUP, GROUP)
            lanes = lane_block(fq * parts + g, LANES)
            weights = [
                wt[d, g, pl.ds(base, GROUP), :].astype(jnp.float32) for d in range(TAPS)
            ]
            for p in range(2):
                acc = [None, None]
                for o in range(TAPS + 8):
                    cell = buf[p, g, pl.ds(base + o, 8), :]
                    for v in range(2):
                        d = o - 8 * v
                        if 0 <= d < TAPS:
                            term = weights[d][8 * v : 8 * v + 8] * cell
                            acc[v] = term if acc[v] is None else acc[v] + term
                value = jnp.concatenate(acc, axis=0).astype(jnp.bfloat16)
                xs[c, p, pl.ds(base, GROUP), lanes] = value

        fq_copy(c, lane_block(fq, freqs)).start()

        @pl.when(c + SLOTS < cuts)
        def _():
            polar_copy(c + SLOTS).start()

    def range_step(c):
        fq_copy(c, lane_block(1 - fq, freqs)).wait_recv()
        dims = (((1,), (1,)), ((), ()))
        table = rtab[...]
        fr = lax.dot_general(table, xs[c, 0], dims, preferred_element_type=jnp.float32)
        fi = lax.dot_general(table, xs[c, 1], dims, preferred_element_type=jnp.float32)
        half = n_az * bins
        scale = 1.0 / math.sqrt(F)
        real = ((fr[:half] - fi[half:]) * scale).astype(jnp.bfloat16)
        imag = ((fr[half:] + fi[:half]) * scale).astype(jnp.bfloat16)
        b, k = c // BATCH, lax.rem(c, BATCH)
        for p, part in enumerate((real, imag)):
            for s in range(n_az):
                piece = part[s * bins : s * bins + late]
                if s == 0:
                    zl[b, p, k, :, own_cols] = piece
                else:
                    rl[c, s - 1, p] = piece
                for g in range(early_groups):
                    at = s * bins + late + g * GROUP
                    er[g, s, 0, p, c] = part[at : at + GROUP]
        for core, shifts in enumerate((order[1:] + order[:1], order)):

            @pl.when(fq == core)
            def _():
                for s in shifts:
                    zl_copy(c, s, own_cols).start()

        for g in range(early_groups - 1):
            xe_copy(c, g).start()

        @pl.when(c < AHEAD)
        def _():
            xe_copy(c, early_groups - 1).start()

    order = list(range(1, n_az))

    def azimuth_tables():
        col = iota((block, A), 1)
        lowc[...], lows[...] = small_trig(iota((block, A), 0) * col, A)
        highc[...], highs[...] = small_trig(iota((A // block, A), 0) * block * col, A)

        @pl.loop(0, A // block)
        def _(i):
            hc, hs = highc[pl.ds(i, 1), :], highs[pl.ds(i, 1), :]
            at = pl.ds(pl.multiple_of(i * block, block), block)
            cos_a[at, :] = (hc * lowc[...] - hs * lows[...]).astype(jnp.bfloat16)
            sin_a[at, :] = (hs * lowc[...] + hc * lows[...]).astype(jnp.bfloat16)

    def height_tables():
        rows, width = 2 * heights, 4 * cuts
        row, col = iota((rows, 128), 0), iota((rows, 128), 1)
        out_imag = row >= heights
        height = el * heights + jnp.where(out_imag, row - heights, row)
        other = col >= 2 * cuts
        inner = jnp.where(other, col - 2 * cuts, col)
        in_imag = inner >= cuts
        source = jnp.where(other, 1 - el, el)
        elev = source * cuts + jnp.where(in_imag, inner - cuts, inner)
        cos_e, sin_e = small_trig(height * elev, E)
        sign = jnp.where(out_imag, sin_e, -sin_e)
        small = jnp.where(out_imag == in_imag, cos_e, sign)
        small = jnp.where(col < width, small, 0.0).astype(jnp.bfloat16)
        tall = rows * GROUP
        take_row = (iota((tall, rows), 0) // GROUP == iota((tall, rows), 1)).astype(
            jnp.bfloat16
        )
        mid = jnp.dot(take_row, small, preferred_element_type=jnp.float32)
        mid = mid.astype(jnp.bfloat16)

        @pl.loop(0, width * GROUP // TILE)
        def _(i):
            shape = (128, TILE)
            col_at = iota(shape, 1) + i * TILE
            take_col = (iota(shape, 0) == col_at // GROUP).astype(jnp.bfloat16)
            spread = jnp.dot(mid, take_col, preferred_element_type=jnp.float32)
            shape = (tall, TILE)
            same = (iota(shape, 0) & (GROUP - 1)) == (iota(shape, 1) & (GROUP - 1))
            htab[:, lane_block(i, TILE)] = jnp.where(same, spread, 0.0).astype(jnp.bfloat16)

    def cross_tile(left, t):
        rows = left.shape[0] // 2
        scale = 1.0 / math.sqrt(A)
        by_cos = jnp.dot(left, cos_a[:, lane_block(t, TILE)], preferred_element_type=jnp.float32)
        by_sin = jnp.dot(left, sin_a[:, lane_block(t, TILE)], preferred_element_type=jnp.float32)
        real = ((by_cos[:rows] - by_sin[rows:]) * scale).astype(jnp.bfloat16)
        imag = ((by_sin[:rows] + by_cos[rows:]) * scale).astype(jnp.bfloat16)
        return real, imag

    def cross_late(b):
        for k in range(BATCH):
            for s in order:
                zl_copy(b * BATCH + k, s, from_az(s)).wait_recv()

        @pl.loop(0, A // TILE)
        def _(t):
            left = zl[b].reshape(2 * BATCH * late, A)
            for p, part in enumerate(cross_tile(left, t)):
                part = part.reshape(BATCH, LATE, GROUP, TILE)
                for g in range(LATE):
                    span = pl.ds(b * BATCH, BATCH)
                    ch[g, 0, p, span, :, lane_block(t, TILE)] = part[:, g]

    def early_heights(g):
        for c in range(cuts):
            xe_copy(c, g).wait_recv()

        @pl.loop(0, n_az)
        def _(s):
            data = er[g, s].reshape(4 * cuts * GROUP, cols)
            total = jnp.dot(htab[...], data, preferred_element_type=jnp.float32)
            total = (total * (1.0 / math.sqrt(E))).astype(jnp.bfloat16)
            total = total.reshape(2, heights, GROUP, cols)

            @pl.when(s == 0)
            def _():
                ez[g, :, :, :, own_cols] = total

            @pl.when(s > 0)
            def _():
                eh[g, s - 1] = total

        for q in range(SPLIT):
            for s in order:
                ze_copy(g, q, s, own_cols).start()

    def cross_early(g, q):
        for s in order:
            ze_copy(g, q, s, from_az(s)).wait_recv()
        some = heights // SPLIT

        @pl.loop(0, A // TILE)
        def _(t):
            left = ez[g, :, q * some : (q + 1) * some].reshape(2 * some * GROUP, A)
            for p, part in enumerate(cross_tile(left, t)):
                at = late + g * GROUP
                out[p, q * some : (q + 1) * some, at : at + GROUP, lane_block(t, TILE)] = (
                    part.reshape(some, GROUP, TILE)
                )

    def late_heights(g, k):
        if g == 0 and k == 0:
            for b in range(batches // 2):
                xa_copy(b).wait_recv()
        for b in range(batches // 2, batches):
            xb_copy(b, g, k).wait_recv()
        some = A // TILE // HALVES

        @pl.loop(k * some, (k + 1) * some)
        def _(t):
            at = lane_block(t, TILE)
            data = ch[g, :, :, :, :, at].reshape(4 * cuts * GROUP, TILE)
            total = jnp.dot(htab[...], data, preferred_element_type=jnp.float32)
            total = (total * (1.0 / math.sqrt(E))).astype(jnp.bfloat16)
            out[:, :, g * GROUP : (g + 1) * GROUP, at] = total.reshape(2, heights, GROUP, TILE)

    def front(first, last):
        @pl.loop(first, last)
        def _(c):
            @pl.when(c < cuts)
            def _():
                interpolate(c)

            @pl.when(c > 0)
            def _():
                range_step(c - 1)

    front(0, cuts + 1)
    for c in range(AHEAD, cuts):
        xe_copy(c, early_groups - 1).start()
    height_tables()
    early_heights(0)
    azimuth_tables()
    cross_late(0)
    xa_copy(0).start()
    cross_late(1)
    xa_copy(1).start()
    for g in range(1, early_groups):
        early_heights(g)
    for b in range(batches // 2, batches):
        cross_late(b)
    for g in range(LATE):
        for k in range(HALVES):
            for b in range(batches // 2, batches):
                xb_copy(b, g, k).start()
    cross_early(0, 0)
    cross_early(0, 1)
    cross_early(1, 0)
    late_heights(0, 0)
    late_heights(0, 1)
    cross_early(1, 1)
    late_heights(1, 0)
    late_heights(1, 1)
    cross_early(2, 0)
    late_heights(2, 0)
    cross_early(2, 1)
    late_heights(2, 1)

    @pl.when(az < n_az - 1)
    def _():
        for k in range(2):
            halo_up(k).wait_send()

    @pl.when(az > 0)
    def _():
        for k in range(2):
            halo_down(k).wait_send()

    @pl.loop(0, cuts)
    def _(c):
        fq_copy(c, lane_block(fq, freqs)).wait_send()
        for s in order:
            zl_copy(c, s, own_cols).wait_send()
        for g in range(early_groups):
            xe_copy(c, g).wait_send()

    for g in range(early_groups):
        for q in range(SPLIT):
            for s in order:
                ze_copy(g, q, s, own_cols).wait_send()
    for b in range(batches // 2):
        xa_copy(b).wait_send()
    for b in range(batches // 2, batches):
        for g in range(LATE):
            for k in range(HALVES):
                xb_copy(b, g, k).wait_send()


def fused(polar, band_offset, tap_count, tap_weight):
    _, cuts, cols, freqs = polar.shape
    n_az = lax.axis_size("az")
    bins = F // (2 * n_az)
    late = LATE * GROUP
    heights = E // 2
    parts = freqs // LANES
    groups = (bins - late) // GROUP
    batches = cuts // BATCH
    far = n_az - 1
    half = jnp.bfloat16
    vmem = pltpu.VMEM
    dma = pltpu.SemaphoreType.DMA
    return pl.pallas_call(
        fused_body,
        out_shape=pltpu.VMEM((2, heights, bins, A), half),
        in_specs=[pl.BlockSpec(memory_space=pl.ANY)] * 4,
        out_specs=pl.BlockSpec(memory_space=pltpu.VMEM),
        scratch_shapes=[
            vmem((cuts, 2, cols, F), half),
            vmem((2, parts, cols + 2 * HW, LANES), jnp.float32),
            vmem((SLOTS, 2, cols, freqs), half),
            vmem((TAPS, parts, cols, LANES), half),
            vmem((cols, freqs), jnp.int32),
            vmem((cols, freqs), jnp.int32),
            vmem((KT, cols, freqs), half),
            vmem((2, cuts, HW, freqs), half),
            vmem((2, cuts, HW, freqs), half),
            vmem((32, A), jnp.float32),
            vmem((32, A), jnp.float32),
            vmem((32, A), jnp.float32),
            vmem((32, A), jnp.float32),
            vmem((2 * n_az * bins, F), half),
            vmem((A, A), half),
            vmem((A, A), half),
            vmem((2 * heights * GROUP, 4 * cuts * GROUP), half),
            vmem((cuts, far, 2, late, cols), half),
            vmem((batches, 2, BATCH, late, A), half),
            vmem((groups, n_az, 2, 2, cuts, GROUP, cols), half),
            vmem((groups, far, 2, heights, GROUP, cols), half),
            vmem((groups, 2, heights, GROUP, A), half),
            vmem((LATE, 2, 2, cuts, GROUP, A), half),
            dma((3,)),
            dma((SLOTS,)),
            dma((2, 2)),
            dma((2, 2)),
            dma((cuts,)),
            dma((cuts,)),
            dma((cuts, far)),
            dma((cuts, far)),
            dma((cuts, groups)),
            dma((cuts, groups)),
            dma((groups, SPLIT, far)),
            dma((groups, SPLIT, far)),
            dma((batches // 2,)),
            dma((batches // 2,)),
            dma((batches // 2, LATE, HALVES)),
            dma((batches // 2, LATE, HALVES)),
        ],
        compiler_params=pltpu.CompilerParams(
            collective_id=0, has_side_effects=True, vmem_limit_bytes=60000000
        ),
        name="image",
    )(polar, band_offset, tap_count, tap_weight)


def pick(polar, band_offset, tap_count, tap_weight):
    _, e_here, col_count, freq_count = polar.shape
    az_count = lax.axis_size("az")
    bins = F // (lax.axis_size("fq") * az_count)
    fits = (
        lax.axis_size("fq") == 2
        and lax.axis_size("el") == 2
        and az_count == 4
        and e_here == 4 * BATCH
        and bins == (LATE + EARLY) * GROUP
        and col_count == TILE
        and freq_count % LANES == 0
    )
    run = fused if fits else on_device
    return run(polar, band_offset, tap_count, tap_weight)


def solution(mesh):
    in_specs = (
        P(None, ("grp", "el"), "az", "fq"),
        P("az", "fq"),
        P("az", "fq"),
        P(None, "az", "fq"),
    )
    out_specs = P(None, ("grp", "el"), ("az", "fq"), None)
    return jax.shard_map(
        pick, mesh=mesh, in_specs=in_specs, out_specs=out_specs, check_vma=False
    )
```

```python
import math

import jax
import jax.numpy as jnp
from jax import lax
from jax.experimental import pallas as pl
from jax.experimental.pallas import tpu as pltpu
from jax.sharding import PartitionSpec as P

F = 768
A = 1024
E = 32
HW = 8
KT = 8
LANES = 128
GROUP = 16
TAPS = 2 * HW + 1
BATCH = 4
LATE = 3
EARLY = 3
AHEAD = 10
HALVES = 4
SLOTS = 4
FIRST = 2
SPLIT = 2
TILE = 256
MESH = pl.DeviceIdType.MESH


def with_halo(cells, sides, width):
    for axis, dim in sides:
        count = lax.axis_size(axis)
        ends = count - 1
        head = lax.slice_in_dim(cells, 0, width, axis=dim)
        tail = lax.slice_in_dim(cells, cells.shape[dim] - width, cells.shape[dim], axis=dim)
        cells = jnp.concatenate(
            [
                lax.ppermute(tail, axis, [(i, (i + 1) % count) for i in range(ends)]),
                cells,
                lax.ppermute(head, axis, [((i + 1) % count, i) for i in range(ends)]),
            ],
            axis=dim,
        )
    return cells


def table_pair(row_ids, col_ids, length):
    product = row_ids[:, None] * col_ids[None, :] % length
    angle = product.astype(jnp.float32) * (2.0 * math.pi / length)
    return (jnp.cos(angle).astype(jnp.bfloat16), jnp.sin(angle).astype(jnp.bfloat16))


def on_device(polar, band_offset, tap_count, tap_weight):
    shape_all = polar.shape
    col_count = shape_all[2]
    freq_count = shape_all[3]
    az_count = lax.axis_size("az")
    fq_count = lax.axis_size("fq")
    el_count = lax.axis_size("el")
    padded = with_halo(polar, (("az", 2),), HW)
    window = col_count + 2 * HW
    column = jnp.arange(col_count, dtype=jnp.int32)[:, None]
    position = jnp.arange(window, dtype=jnp.int32)[None, :, None]
    band_matrix = jnp.zeros((col_count, window, freq_count), jnp.bfloat16)
    for tap_index in range(KT):
        reach = column + HW + band_offset + tap_index
        matches = (position == reach[:, None, :]) & (tap_index < tap_count)[:, None, :]
        band_matrix = jnp.where(matches, tap_weight[tap_index][:, None, :], band_matrix)
    interpolated = jnp.einsum(
        "jaf,ceaf->cejf", band_matrix, padded, preferred_element_type=jnp.float32
    ).astype(jnp.bfloat16)
    fq_index = lax.axis_index("fq")
    bin_count = F // (fq_count * az_count)
    az_block = jnp.arange(az_count, dtype=jnp.int32)[:, None]
    bin_local = jnp.arange(bin_count, dtype=jnp.int32)[None, :]
    range_bins = ((az_block * fq_count + fq_index) * bin_count + bin_local).reshape(-1)
    cos_f, sin_f = table_pair(jnp.arange(F, dtype=jnp.int32), range_bins, F)
    shard_piece = lax.all_gather(interpolated, "fq", axis=3, tiled=True)
    cos_rows = cos_f
    sin_rows = sin_f
    real_part = jnp.einsum(
        "ejf,fk->ekj", shard_piece[0], cos_rows, preferred_element_type=jnp.float32
    ) - jnp.einsum("ejf,fk->ekj", shard_piece[1], sin_rows, preferred_element_type=jnp.float32)
    imag_part = jnp.einsum(
        "ejf,fk->ekj", shard_piece[0], sin_rows, preferred_element_type=jnp.float32
    ) + jnp.einsum("ejf,fk->ekj", shard_piece[1], cos_rows, preferred_element_type=jnp.float32)
    summed = jnp.stack([real_part, imag_part])
    ranged = (summed * (1.0 / math.sqrt(F))).astype(jnp.bfloat16)
    azim_ids = jnp.arange(A, dtype=jnp.int32)
    cos_a, sin_a = table_pair(azim_ids, azim_ids, A)
    block_data = lax.all_to_all(ranged, "az", split_axis=2, concat_axis=3, tiled=True)
    real_part = jnp.einsum(
        "ekj,jm->ekm", block_data[0], cos_a, preferred_element_type=jnp.float32
    ) - jnp.einsum("ekj,jm->ekm", block_data[1], sin_a, preferred_element_type=jnp.float32)
    imag_part = jnp.einsum(
        "ekj,jm->ekm", block_data[0], sin_a, preferred_element_type=jnp.float32
    ) + jnp.einsum("ekj,jm->ekm", block_data[1], cos_a, preferred_element_type=jnp.float32)
    crossed = (jnp.stack([real_part, imag_part]) * (1.0 / math.sqrt(A))).astype(jnp.bfloat16)
    elev_ids = jnp.arange(E, dtype=jnp.int32)
    el_index = lax.axis_index("el")
    height_count = E // el_count
    height_rows = el_index * height_count + jnp.arange(height_count, dtype=jnp.int32)
    cos_e, sin_e = table_pair(elev_ids, height_rows, E)
    shard_piece = lax.all_gather(crossed, "el", axis=1, tiled=True)
    cos_rows = cos_e
    sin_rows = sin_e
    real_part = jnp.einsum(
        "eh,ekm->hkm", cos_rows, shard_piece[0], preferred_element_type=jnp.float32
    ) - jnp.einsum("eh,ekm->hkm", sin_rows, shard_piece[1], preferred_element_type=jnp.float32)
    imag_part = jnp.einsum(
        "eh,ekm->hkm", sin_rows, shard_piece[0], preferred_element_type=jnp.float32
    ) + jnp.einsum("eh,ekm->hkm", cos_rows, shard_piece[1], preferred_element_type=jnp.float32)
    totals = jnp.stack([real_part, imag_part])
    image_out = (totals * (1.0 / math.sqrt(E))).astype(jnp.bfloat16)
    return image_out


def small_trig(product, length):
    value = product.astype(jnp.float32)
    turns = jnp.floor(value * (1.0 / length))
    angle = (value - turns * length) * (2.0 * math.pi / length)
    return jnp.cos(angle), jnp.sin(angle)


def iota(shape, dim):
    return lax.broadcasted_iota(jnp.int32, shape, dim)


def fused_body(
    polar, off_h, cnt_h, tap_h, out,
    xs, buf, pv, wt, offv, cntv, tapv, hl, hr,
    lowc, lows, highc, highs, rtab, cos_a, sin_a, htab,
    rl, zl, er, eh, ez, ch,
    in_sem, pv_sem, halo_s, halo_r, fq_s, fq_r, zl_s, zl_r,
    xe_s, xe_r, ze_s, ze_r, xa_s, xa_r, xb_s, xb_r,
):
    n_az = lax.axis_size("az")
    az, fq, el = (lax.axis_index(name) for name in ("az", "fq", "el"))
    _, cuts, cols, freqs = polar.shape
    parts = freqs // LANES
    heights = E // 2
    late = LATE * GROUP
    bins = out.shape[2]
    early_groups = (bins - late) // GROUP
    batches = cuts // BATCH
    steps = cols // GROUP

    def at_az(shift):
        return {"az": lax.rem(az + shift, n_az)}

    def lane_block(index, size):
        return pl.ds(pl.multiple_of(index * size, LANES), size)

    fq_peer = {"fq": 1 - fq}
    el_peer = {"el": 1 - el}
    own_cols = lane_block(az, cols)

    def from_az(shift):
        return lane_block(lax.rem(az - shift + n_az, n_az), cols)

    def remote(source, target, send, recv, where):
        return pltpu.make_async_remote_copy(
            src_ref=source,
            dst_ref=target,
            send_sem=send,
            recv_sem=recv,
            device_id=where,
            device_id_type=MESH,
        )

    def polar_copy(c):
        slot = lax.rem(c, SLOTS)
        return pltpu.make_async_copy(polar.at[:, c], pv.at[slot], pv_sem.at[slot])

    spans = (pl.ds(0, FIRST), pl.ds(FIRST, cuts - FIRST))

    def halo_up(k):
        return remote(
            polar.at[:, spans[k], pl.ds(cols - HW, HW)],
            hl.at[:, spans[k]],
            halo_s.at[0, k],
            halo_r.at[0, k],
            at_az(1),
        )

    def halo_down(k):
        return remote(
            polar.at[:, spans[k], pl.ds(0, HW)],
            hr.at[:, spans[k]],
            halo_s.at[1, k],
            halo_r.at[1, k],
            at_az(n_az - 1),
        )

    def fq_copy(c, lanes):
        return remote(
            xs.at[c, :, :, lanes], xs.at[c, :, :, lanes], fq_s.at[c], fq_r.at[c], fq_peer
        )

    def zl_copy(c, shift, lanes):
        return remote(
            rl.at[c, shift - 1],
            zl.at[c // BATCH, :, lax.rem(c, BATCH), :, lanes],
            zl_s.at[c, shift - 1],
            zl_r.at[c, shift - 1],
            at_az(shift),
        )

    def xe_copy(c, g):
        return remote(
            er.at[g, :, 0, :, c],
            er.at[g, :, 1, :, c],
            xe_s.at[c, g],
            xe_r.at[c, g],
            el_peer,
        )

    def ze_copy(g, q, shift, lanes):
        span = pl.ds(q * (heights // SPLIT), heights // SPLIT)
        return remote(
            eh.at[g, shift - 1, :, span],
            ez.at[g, :, span, :, lanes],
            ze_s.at[g, q, shift - 1],
            ze_r.at[g, q, shift - 1],
            at_az(shift),
        )

    def xa_copy(b):
        span = pl.ds(b * BATCH, BATCH)
        return remote(
            ch.at[:, 0, :, span], ch.at[:, 1, :, span], xa_s.at[b], xa_r.at[b], el_peer
        )

    def xb_copy(b, g, k):
        span = pl.ds(b * BATCH, BATCH)
        half = batches // 2
        lanes = pl.ds(k * (A // HALVES), A // HALVES)
        return remote(
            ch.at[g, 0, :, span, :, lanes],
            ch.at[g, 1, :, span, :, lanes],
            xb_s.at[b - half, g, k],
            xb_r.at[b - half, g, k],
            el_peer,
        )

    barrier = pltpu.get_barrier_semaphore()
    peers = [fq_peer, el_peer] + [at_az(s) for s in range(1, n_az)]
    for peer in peers:
        pl.semaphore_signal(barrier, inc=1, device_id=peer, device_id_type=MESH)
    loads = [
        pltpu.make_async_copy(off_h, offv, in_sem.at[0]),
        pltpu.make_async_copy(cnt_h, cntv, in_sem.at[1]),
        pltpu.make_async_copy(tap_h, tapv, in_sem.at[2]),
    ]
    for load in loads:
        load.start()
    for c in range(SLOTS):
        polar_copy(c).start()

    @pl.when(az == 0)
    def _():
        hl[...] = jnp.zeros(hl.shape, hl.dtype)

    @pl.when(az == n_az - 1)
    def _():
        hr[...] = jnp.zeros(hr.shape, hr.dtype)

    pl.semaphore_wait(barrier, len(peers))

    @pl.when(az < n_az - 1)
    def _():
        for k in range(2):
            halo_up(k).start()

    @pl.when(az > 0)
    def _():
        for k in range(2):
            halo_down(k).start()

    block = 32
    blocks = n_az * bins // block
    per = bins // block
    row = iota((16, F), 0)
    shift = jnp.zeros((16, F), jnp.int32)
    for s in range(1, n_az):
        shift = shift + (row >= s * per).astype(jnp.int32)
    inner = row - shift * per
    target = az + shift
    target = jnp.where(target >= n_az, target - n_az, target)
    starts = (target * 2 + fq) * bins + inner * block
    wide = slice(0, F)
    highc[0:16, wide], highs[0:16, wide] = small_trig(starts * iota((16, F), 1), F)
    lowc[:, wide], lows[:, wide] = small_trig(iota((block, F), 0) * iota((block, F), 1), F)

    @pl.loop(0, blocks)
    def _(i):
        hc, hs = highc[pl.ds(i, 1), wide], highs[pl.ds(i, 1), wide]
        lc, ls = lowc[:, wide], lows[:, wide]
        at = pl.ds(pl.multiple_of(i * block, block), block)
        rtab[at, :] = (hc * lc - hs * ls).astype(jnp.bfloat16)
        at = pl.ds(pl.multiple_of((blocks + i) * block, block), block)
        rtab[at, :] = (hs * lc + hc * ls).astype(jnp.bfloat16)

    for load in loads:
        load.wait()

    @pl.loop(0, parts * steps)
    def _(i):
        g = i // steps
        rows = pl.ds(pl.multiple_of(lax.rem(i, steps) * GROUP, GROUP), GROUP)
        lanes = lane_block(g, LANES)
        rel = offv[rows, lanes] + HW
        cnt = cntv[rows, lanes]
        zero = jnp.zeros(rel.shape, jnp.float32)
        taps = [
            jnp.where(t < cnt, tapv[t, rows, lanes].astype(jnp.float32), zero)
            for t in range(KT)
        ]
        for bit in range(4):
            step = 1 << bit
            on = (rel & step) != 0
            size = min(TAPS, len(taps) + step)
            taps = [
                jnp.where(
                    on,
                    taps[d - step] if d >= step else zero,
                    taps[d] if d < len(taps) else zero,
                )
                for d in range(size)
            ]
        for d in range(TAPS):
            wt[d, g, rows, :] = taps[d].astype(jnp.bfloat16)

    def wait_halo(k):
        @pl.when(az > 0)
        def _():
            halo_up(k).wait_recv()

        @pl.when(az < n_az - 1)
        def _():
            halo_down(k).wait_recv()

    def interpolate(c):
        slot = lax.rem(c, SLOTS)
        polar_copy(c).wait()
        for p in range(2):
            for g in range(parts):
                lanes = slice(g * LANES, (g + 1) * LANES)
                buf[p, g, HW : HW + cols, :] = pv[slot, p, :, lanes].astype(jnp.float32)

        def combine(g, r):
            base = pl.multiple_of(r * GROUP, GROUP)
            lanes = lane_block(fq * parts + g, LANES)
            weights = [
                wt[d, g, pl.ds(base, GROUP), :].astype(jnp.float32) for d in range(TAPS)
            ]
            for p in range(2):
                acc = [None, None]
                for o in range(TAPS + 8):
                    cell = buf[p, g, pl.ds(base + o, 8), :]
                    for v in range(2):
                        d = o - 8 * v
                        if 0 <= d < TAPS:
                            term = weights[d][8 * v : 8 * v + 8] * cell
                            acc[v] = term if acc[v] is None else acc[v] + term
                value = jnp.concatenate(acc, axis=0).astype(jnp.bfloat16)
                xs[c, p, pl.ds(base, GROUP), lanes] = value

        inside = steps - 2

        @pl.loop(0, parts * inside)
        def _(i):
            combine(i // inside, 1 + lax.rem(i, inside))

        @pl.when(c == 0)
        def _():
            wait_halo(0)

        @pl.when(c == FIRST)
        def _():
            wait_halo(1)

        for p in range(2):
            for g in range(parts):
                lanes = slice(g * LANES, (g + 1) * LANES)
                buf[p, g, 0:HW, :] = hl[p, c, :, lanes].astype(jnp.float32)
                buf[p, g, HW + cols :, :] = hr[p, c, :, lanes].astype(jnp.float32)

        @pl.loop(0, parts * 2)
        def _(i):
            combine(i // 2, lax.rem(i, 2) * (steps - 1))

        fq_copy(c, lane_block(fq, freqs)).start()

        @pl.when(c + SLOTS < cuts)
        def _():
            polar_copy(c + SLOTS).start()

    def range_step(c):
        fq_copy(c, lane_block(1 - fq, freqs)).wait_recv()
        dims = (((1,), (1,)), ((), ()))
        table = rtab[...]
        fr = lax.dot_general(table, xs[c, 0], dims, preferred_element_type=jnp.float32)
        fi = lax.dot_general(table, xs[c, 1], dims, preferred_element_type=jnp.float32)
        half = n_az * bins
        scale = 1.0 / math.sqrt(F)
        real = ((fr[:half] - fi[half:]) * scale).astype(jnp.bfloat16)
        imag = ((fr[half:] + fi[:half]) * scale).astype(jnp.bfloat16)
        b, k = c // BATCH, lax.rem(c, BATCH)
        for p, part in enumerate((real, imag)):
            for s in range(n_az):
                piece = part[s * bins : s * bins + late]
                if s == 0:
                    zl[b, p, k, :, own_cols] = piece
                else:
                    rl[c, s - 1, p] = piece
                for g in range(early_groups):
                    at = s * bins + late + g * GROUP
                    er[g, s, 0, p, c] = part[at : at + GROUP]
        for core, shifts in enumerate((order[1:] + order[:1], order)):

            @pl.when(fq == core)
            def _():
                for s in shifts:
                    zl_copy(c, s, own_cols).start()

        for g in range(early_groups - 1):
            xe_copy(c, g).start()

        @pl.when(c < AHEAD)
        def _():
            xe_copy(c, early_groups - 1).start()

    order = list(range(1, n_az))

    def azimuth_tables():
        col = iota((block, A), 1)
        lowc[...], lows[...] = small_trig(iota((block, A), 0) * col, A)
        highc[...], highs[...] = small_trig(iota((A // block, A), 0) * block * col, A)

        @pl.loop(0, A // block)
        def _(i):
            hc, hs = highc[pl.ds(i, 1), :], highs[pl.ds(i, 1), :]
            at = pl.ds(pl.multiple_of(i * block, block), block)
            cos_a[at, :] = (hc * lowc[...] - hs * lows[...]).astype(jnp.bfloat16)
            sin_a[at, :] = (hs * lowc[...] + hc * lows[...]).astype(jnp.bfloat16)

    def height_tables():
        rows, width = 2 * heights, 4 * cuts
        row, col = iota((rows, 128), 0), iota((rows, 128), 1)
        out_imag = row >= heights
        height = el * heights + jnp.where(out_imag, row - heights, row)
        other = col >= 2 * cuts
        inner = jnp.where(other, col - 2 * cuts, col)
        in_imag = inner >= cuts
        source = jnp.where(other, 1 - el, el)
        elev = source * cuts + jnp.where(in_imag, inner - cuts, inner)
        cos_e, sin_e = small_trig(height * elev, E)
        sign = jnp.where(out_imag, sin_e, -sin_e)
        small = jnp.where(out_imag == in_imag, cos_e, sign)
        small = jnp.where(col < width, small, 0.0).astype(jnp.bfloat16)
        tall = rows * GROUP
        take_row = (iota((tall, rows), 0) // GROUP == iota((tall, rows), 1)).astype(
            jnp.bfloat16
        )
        mid = jnp.dot(take_row, small, preferred_element_type=jnp.float32)
        mid = mid.astype(jnp.bfloat16)

        @pl.loop(0, width * GROUP // TILE)
        def _(i):
            shape = (128, TILE)
            col_at = iota(shape, 1) + i * TILE
            take_col = (iota(shape, 0) == col_at // GROUP).astype(jnp.bfloat16)
            spread = jnp.dot(mid, take_col, preferred_element_type=jnp.float32)
            shape = (tall, TILE)
            same = (iota(shape, 0) & (GROUP - 1)) == (iota(shape, 1) & (GROUP - 1))
            htab[:, lane_block(i, TILE)] = jnp.where(same, spread, 0.0).astype(jnp.bfloat16)

    def cross_tile(left, t):
        rows = left.shape[0] // 2
        scale = 1.0 / math.sqrt(A)
        by_cos = jnp.dot(left, cos_a[:, lane_block(t, TILE)], preferred_element_type=jnp.float32)
        by_sin = jnp.dot(left, sin_a[:, lane_block(t, TILE)], preferred_element_type=jnp.float32)
        real = ((by_cos[:rows] - by_sin[rows:]) * scale).astype(jnp.bfloat16)
        imag = ((by_sin[:rows] + by_cos[rows:]) * scale).astype(jnp.bfloat16)
        return real, imag

    def cross_late(b):
        for k in range(BATCH):
            for s in order:
                zl_copy(b * BATCH + k, s, from_az(s)).wait_recv()

        @pl.loop(0, A // TILE)
        def _(t):
            left = zl[b].reshape(2 * BATCH * late, A)
            for p, part in enumerate(cross_tile(left, t)):
                part = part.reshape(BATCH, LATE, GROUP, TILE)
                for g in range(LATE):
                    span = pl.ds(b * BATCH, BATCH)
                    ch[g, 0, p, span, :, lane_block(t, TILE)] = part[:, g]

    def early_heights(g):
        for c in range(cuts):
            xe_copy(c, g).wait_recv()

        @pl.loop(0, n_az)
        def _(s):
            data = er[g, s].reshape(4 * cuts * GROUP, cols)
            total = jnp.dot(htab[...], data, preferred_element_type=jnp.float32)
            total = (total * (1.0 / math.sqrt(E))).astype(jnp.bfloat16)
            total = total.reshape(2, heights, GROUP, cols)

            @pl.when(s == 0)
            def _():
                ez[g, :, :, :, own_cols] = total

            @pl.when(s > 0)
            def _():
                eh[g, s - 1] = total

        for q in range(SPLIT):
            for s in order:
                ze_copy(g, q, s, own_cols).start()

    def cross_early(g, q):
        for s in order:
            ze_copy(g, q, s, from_az(s)).wait_recv()
        some = heights // SPLIT

        @pl.loop(0, A // TILE)
        def _(t):
            left = ez[g, :, q * some : (q + 1) * some].reshape(2 * some * GROUP, A)
            for p, part in enumerate(cross_tile(left, t)):
                at = late + g * GROUP
                out[p, q * some : (q + 1) * some, at : at + GROUP, lane_block(t, TILE)] = (
                    part.reshape(some, GROUP, TILE)
                )

    def late_heights(g, k):
        if g == 0 and k == 0:
            for b in range(batches // 2):
                xa_copy(b).wait_recv()
        for b in range(batches // 2, batches):
            xb_copy(b, g, k).wait_recv()
        some = A // TILE // HALVES

        @pl.loop(k * some, (k + 1) * some)
        def _(t):
            at = lane_block(t, TILE)
            data = ch[g, :, :, :, :, at].reshape(4 * cuts * GROUP, TILE)
            total = jnp.dot(htab[...], data, preferred_element_type=jnp.float32)
            total = (total * (1.0 / math.sqrt(E))).astype(jnp.bfloat16)
            out[:, :, g * GROUP : (g + 1) * GROUP, at] = total.reshape(2, heights, GROUP, TILE)

    def front(first, last):
        @pl.loop(first, last)
        def _(c):
            @pl.when(c < cuts)
            def _():
                interpolate(c)

            @pl.when(c > 0)
            def _():
                range_step(c - 1)

    front(0, cuts + 1)
    for c in range(AHEAD, cuts):
        xe_copy(c, early_groups - 1).start()
    azimuth_tables()
    cross_late(0)
    xa_copy(0).start()
    height_tables()
    early_heights(0)
    cross_late(1)
    xa_copy(1).start()
    for g in range(1, early_groups):
        early_heights(g)
    for b in range(batches // 2, batches):
        cross_late(b)
    for g in range(LATE):
        for k in range(HALVES):
            for b in range(batches // 2, batches):
                xb_copy(b, g, k).start()
    cross_early(0, 0)
    cross_early(0, 1)
    cross_early(1, 0)
    for k in range(HALVES):
        late_heights(0, k)
    cross_early(1, 1)
    for k in range(HALVES):
        late_heights(1, k)
    cross_early(2, 0)
    for k in range(HALVES - 1):
        late_heights(2, k)
    cross_early(2, 1)
    late_heights(2, HALVES - 1)

    @pl.when(az < n_az - 1)
    def _():
        for k in range(2):
            halo_up(k).wait_send()

    @pl.when(az > 0)
    def _():
        for k in range(2):
            halo_down(k).wait_send()

    @pl.loop(0, cuts)
    def _(c):
        fq_copy(c, lane_block(fq, freqs)).wait_send()
        for s in order:
            zl_copy(c, s, own_cols).wait_send()
        for g in range(early_groups):
            xe_copy(c, g).wait_send()

    for g in range(early_groups):
        for q in range(SPLIT):
            for s in order:
                ze_copy(g, q, s, own_cols).wait_send()
    for b in range(batches // 2):
        xa_copy(b).wait_send()
    for b in range(batches // 2, batches):
        for g in range(LATE):
            for k in range(HALVES):
                xb_copy(b, g, k).wait_send()


def fused(polar, band_offset, tap_count, tap_weight):
    _, cuts, cols, freqs = polar.shape
    n_az = lax.axis_size("az")
    bins = F // (2 * n_az)
    late = LATE * GROUP
    heights = E // 2
    parts = freqs // LANES
    groups = (bins - late) // GROUP
    batches = cuts // BATCH
    far = n_az - 1
    half = jnp.bfloat16
    vmem = pltpu.VMEM
    dma = pltpu.SemaphoreType.DMA
    return pl.pallas_call(
        fused_body,
        out_shape=pltpu.VMEM((2, heights, bins, A), half),
        in_specs=[pl.BlockSpec(memory_space=pl.ANY)] * 4,
        out_specs=pl.BlockSpec(memory_space=pltpu.VMEM),
        scratch_shapes=[
            vmem((cuts, 2, cols, F), half),
            vmem((2, parts, cols + 2 * HW, LANES), jnp.float32),
            vmem((SLOTS, 2, cols, freqs), half),
            vmem((TAPS, parts, cols, LANES), half),
            vmem((cols, freqs), jnp.int32),
            vmem((cols, freqs), jnp.int32),
            vmem((KT, cols, freqs), half),
            vmem((2, cuts, HW, freqs), half),
            vmem((2, cuts, HW, freqs), half),
            vmem((32, A), jnp.float32),
            vmem((32, A), jnp.float32),
            vmem((32, A), jnp.float32),
            vmem((32, A), jnp.float32),
            vmem((2 * n_az * bins, F), half),
            vmem((A, A), half),
            vmem((A, A), half),
            vmem((2 * heights * GROUP, 4 * cuts * GROUP), half),
            vmem((cuts, far, 2, late, cols), half),
            vmem((batches, 2, BATCH, late, A), half),
            vmem((groups, n_az, 2, 2, cuts, GROUP, cols), half),
            vmem((groups, far, 2, heights, GROUP, cols), half),
            vmem((groups, 2, heights, GROUP, A), half),
            vmem((LATE, 2, 2, cuts, GROUP, A), half),
            dma((3,)),
            dma((SLOTS,)),
            dma((2, 2)),
            dma((2, 2)),
            dma((cuts,)),
            dma((cuts,)),
            dma((cuts, far)),
            dma((cuts, far)),
            dma((cuts, groups)),
            dma((cuts, groups)),
            dma((groups, SPLIT, far)),
            dma((groups, SPLIT, far)),
            dma((batches // 2,)),
            dma((batches // 2,)),
            dma((batches // 2, LATE, HALVES)),
            dma((batches // 2, LATE, HALVES)),
        ],
        compiler_params=pltpu.CompilerParams(
            collective_id=0, has_side_effects=True, vmem_limit_bytes=60000000
        ),
        name="image",
    )(polar, band_offset, tap_count, tap_weight)


def pick(polar, band_offset, tap_count, tap_weight):
    _, e_here, col_count, freq_count = polar.shape
    az_count = lax.axis_size("az")
    bins = F // (lax.axis_size("fq") * az_count)
    fits = (
        lax.axis_size("fq") == 2
        and lax.axis_size("el") == 2
        and az_count == 4
        and e_here == 4 * BATCH
        and bins == (LATE + EARLY) * GROUP
        and col_count == TILE
        and freq_count % LANES == 0
    )
    run = fused if fits else on_device
    return run(polar, band_offset, tap_count, tap_weight)


def solution(mesh):
    in_specs = (
        P(None, ("grp", "el"), "az", "fq"),
        P("az", "fq"),
        P("az", "fq"),
        P(None, "az", "fq"),
    )
    out_specs = P(None, ("grp", "el"), ("az", "fq"), None)
    return jax.shard_map(
        pick, mesh=mesh, in_specs=in_specs, out_specs=out_specs, check_vma=False
    )
```

```python
import math

import jax
import jax.numpy as jnp
from jax import lax
from jax.experimental import pallas as pl
from jax.experimental.pallas import tpu as pltpu
from jax.sharding import PartitionSpec as P

F = 768
A = 1024
E = 32
HW = 8
KT = 8
LANES = 128
GROUP = 16
TAPS = 2 * HW + 1
BATCH = 4
LATE = 3
EARLY = 3
AHEAD = 10
HALVES = 2
SLOTS = 4
FIRST = 2
SPLIT = 2
TILE = 256
MESH = pl.DeviceIdType.MESH


def with_halo(cells, sides, width):
    for axis, dim in sides:
        count = lax.axis_size(axis)
        ends = count - 1
        head = lax.slice_in_dim(cells, 0, width, axis=dim)
        tail = lax.slice_in_dim(cells, cells.shape[dim] - width, cells.shape[dim], axis=dim)
        cells = jnp.concatenate(
            [
                lax.ppermute(tail, axis, [(i, (i + 1) % count) for i in range(ends)]),
                cells,
                lax.ppermute(head, axis, [((i + 1) % count, i) for i in range(ends)]),
            ],
            axis=dim,
        )
    return cells


def table_pair(row_ids, col_ids, length):
    product = row_ids[:, None] * col_ids[None, :] % length
    angle = product.astype(jnp.float32) * (2.0 * math.pi / length)
    return (jnp.cos(angle).astype(jnp.bfloat16), jnp.sin(angle).astype(jnp.bfloat16))


def on_device(polar, band_offset, tap_count, tap_weight):
    shape_all = polar.shape
    col_count = shape_all[2]
    freq_count = shape_all[3]
    az_count = lax.axis_size("az")
    fq_count = lax.axis_size("fq")
    el_count = lax.axis_size("el")
    padded = with_halo(polar, (("az", 2),), HW)
    window = col_count + 2 * HW
    column = jnp.arange(col_count, dtype=jnp.int32)[:, None]
    position = jnp.arange(window, dtype=jnp.int32)[None, :, None]
    band_matrix = jnp.zeros((col_count, window, freq_count), jnp.bfloat16)
    for tap_index in range(KT):
        reach = column + HW + band_offset + tap_index
        matches = (position == reach[:, None, :]) & (tap_index < tap_count)[:, None, :]
        band_matrix = jnp.where(matches, tap_weight[tap_index][:, None, :], band_matrix)
    interpolated = jnp.einsum(
        "jaf,ceaf->cejf", band_matrix, padded, preferred_element_type=jnp.float32
    ).astype(jnp.bfloat16)
    fq_index = lax.axis_index("fq")
    bin_count = F // (fq_count * az_count)
    az_block = jnp.arange(az_count, dtype=jnp.int32)[:, None]
    bin_local = jnp.arange(bin_count, dtype=jnp.int32)[None, :]
    range_bins = ((az_block * fq_count + fq_index) * bin_count + bin_local).reshape(-1)
    cos_f, sin_f = table_pair(jnp.arange(F, dtype=jnp.int32), range_bins, F)
    shard_piece = lax.all_gather(interpolated, "fq", axis=3, tiled=True)
    cos_rows = cos_f
    sin_rows = sin_f
    real_part = jnp.einsum(
        "ejf,fk->ekj", shard_piece[0], cos_rows, preferred_element_type=jnp.float32
    ) - jnp.einsum("ejf,fk->ekj", shard_piece[1], sin_rows, preferred_element_type=jnp.float32)
    imag_part = jnp.einsum(
        "ejf,fk->ekj", shard_piece[0], sin_rows, preferred_element_type=jnp.float32
    ) + jnp.einsum("ejf,fk->ekj", shard_piece[1], cos_rows, preferred_element_type=jnp.float32)
    summed = jnp.stack([real_part, imag_part])
    ranged = (summed * (1.0 / math.sqrt(F))).astype(jnp.bfloat16)
    azim_ids = jnp.arange(A, dtype=jnp.int32)
    cos_a, sin_a = table_pair(azim_ids, azim_ids, A)
    block_data = lax.all_to_all(ranged, "az", split_axis=2, concat_axis=3, tiled=True)
    real_part = jnp.einsum(
        "ekj,jm->ekm", block_data[0], cos_a, preferred_element_type=jnp.float32
    ) - jnp.einsum("ekj,jm->ekm", block_data[1], sin_a, preferred_element_type=jnp.float32)
    imag_part = jnp.einsum(
        "ekj,jm->ekm", block_data[0], sin_a, preferred_element_type=jnp.float32
    ) + jnp.einsum("ekj,jm->ekm", block_data[1], cos_a, preferred_element_type=jnp.float32)
    crossed = (jnp.stack([real_part, imag_part]) * (1.0 / math.sqrt(A))).astype(jnp.bfloat16)
    elev_ids = jnp.arange(E, dtype=jnp.int32)
    el_index = lax.axis_index("el")
    height_count = E // el_count
    height_rows = el_index * height_count + jnp.arange(height_count, dtype=jnp.int32)
    cos_e, sin_e = table_pair(elev_ids, height_rows, E)
    shard_piece = lax.all_gather(crossed, "el", axis=1, tiled=True)
    cos_rows = cos_e
    sin_rows = sin_e
    real_part = jnp.einsum(
        "eh,ekm->hkm", cos_rows, shard_piece[0], preferred_element_type=jnp.float32
    ) - jnp.einsum("eh,ekm->hkm", sin_rows, shard_piece[1], preferred_element_type=jnp.float32)
    imag_part = jnp.einsum(
        "eh,ekm->hkm", sin_rows, shard_piece[0], preferred_element_type=jnp.float32
    ) + jnp.einsum("eh,ekm->hkm", cos_rows, shard_piece[1], preferred_element_type=jnp.float32)
    totals = jnp.stack([real_part, imag_part])
    image_out = (totals * (1.0 / math.sqrt(E))).astype(jnp.bfloat16)
    return image_out


def small_trig(product, length):
    value = product.astype(jnp.float32)
    turns = jnp.floor(value * (1.0 / length))
    angle = (value - turns * length) * (2.0 * math.pi / length)
    return jnp.cos(angle), jnp.sin(angle)


def iota(shape, dim):
    return lax.broadcasted_iota(jnp.int32, shape, dim)


def fused_body(
    polar, off_h, cnt_h, tap_h, out,
    xs, buf, pv, wt, offv, cntv, tapv, hl, hr,
    lowc, lows, highc, highs, rtab, cos_a, sin_a, htab,
    rl, zl, er, eh, ez, ch,
    in_sem, pv_sem, halo_s, halo_r, fq_s, fq_r, zl_s, zl_r,
    xe_s, xe_r, ze_s, ze_r, xa_s, xa_r, xb_s, xb_r,
):
    n_az = lax.axis_size("az")
    az, fq, el = (lax.axis_index(name) for name in ("az", "fq", "el"))
    _, cuts, cols, freqs = polar.shape
    parts = freqs // LANES
    heights = E // 2
    late = LATE * GROUP
    bins = out.shape[2]
    early_groups = (bins - late) // GROUP
    batches = cuts // BATCH
    steps = cols // GROUP

    def at_az(shift):
        return {"az": lax.rem(az + shift, n_az)}

    def lane_block(index, size):
        return pl.ds(pl.multiple_of(index * size, LANES), size)

    fq_peer = {"fq": 1 - fq}
    el_peer = {"el": 1 - el}
    own_cols = lane_block(az, cols)

    def from_az(shift):
        return lane_block(lax.rem(az - shift + n_az, n_az), cols)

    def remote(source, target, send, recv, where):
        return pltpu.make_async_remote_copy(
            src_ref=source,
            dst_ref=target,
            send_sem=send,
            recv_sem=recv,
            device_id=where,
            device_id_type=MESH,
        )

    def polar_copy(c):
        slot = lax.rem(c, SLOTS)
        return pltpu.make_async_copy(polar.at[:, c], pv.at[slot], pv_sem.at[slot])

    spans = (pl.ds(0, FIRST), pl.ds(FIRST, cuts - FIRST))

    def halo_up(k):
        return remote(
            polar.at[:, spans[k], pl.ds(cols - HW, HW)],
            hl.at[:, spans[k]],
            halo_s.at[0, k],
            halo_r.at[0, k],
            at_az(1),
        )

    def halo_down(k):
        return remote(
            polar.at[:, spans[k], pl.ds(0, HW)],
            hr.at[:, spans[k]],
            halo_s.at[1, k],
            halo_r.at[1, k],
            at_az(n_az - 1),
        )

    def fq_copy(c, lanes):
        return remote(
            xs.at[c, :, :, lanes], xs.at[c, :, :, lanes], fq_s.at[c], fq_r.at[c], fq_peer
        )

    def zl_copy(c, shift, lanes):
        return remote(
            rl.at[c, shift - 1],
            zl.at[c // BATCH, :, lax.rem(c, BATCH), :, lanes],
            zl_s.at[c, shift - 1],
            zl_r.at[c, shift - 1],
            at_az(shift),
        )

    def xe_copy(c, g):
        return remote(
            er.at[g, 0, c],
            er.at[g, 1, c],
            xe_s.at[c, g],
            xe_r.at[c, g],
            el_peer,
        )

    def ze_copy(g, q, shift, lanes):
        span = pl.ds(q * (heights // SPLIT), heights // SPLIT)
        return remote(
            eh.at[g, shift - 1, :, span],
            ez.at[g, :, span, :, lanes],
            ze_s.at[g, q, shift - 1],
            ze_r.at[g, q, shift - 1],
            at_az(shift),
        )

    def xa_copy(b):
        span = pl.ds(b * BATCH, BATCH)
        return remote(
            ch.at[:, 0, span], ch.at[:, 1, span], xa_s.at[b], xa_r.at[b], el_peer
        )

    def xb_copy(b, g, k):
        span = pl.ds(b * BATCH, BATCH)
        half = batches // 2
        lanes = pl.ds(k * (A // HALVES), A // HALVES)
        return remote(
            ch.at[g, 0, span, :, :, lanes],
            ch.at[g, 1, span, :, :, lanes],
            xb_s.at[b - half, g, k],
            xb_r.at[b - half, g, k],
            el_peer,
        )

    barrier = pltpu.get_barrier_semaphore()
    peers = [fq_peer, el_peer] + [at_az(s) for s in range(1, n_az)]
    for peer in peers:
        pl.semaphore_signal(barrier, inc=1, device_id=peer, device_id_type=MESH)
    loads = [
        pltpu.make_async_copy(off_h, offv, in_sem.at[0]),
        pltpu.make_async_copy(cnt_h, cntv, in_sem.at[1]),
        pltpu.make_async_copy(tap_h, tapv, in_sem.at[2]),
    ]
    for load in loads:
        load.start()
    for c in range(SLOTS):
        polar_copy(c).start()

    @pl.when(az == 0)
    def _():
        hl[...] = jnp.zeros(hl.shape, hl.dtype)

    @pl.when(az == n_az - 1)
    def _():
        hr[...] = jnp.zeros(hr.shape, hr.dtype)

    pl.semaphore_wait(barrier, len(peers))

    @pl.when(az < n_az - 1)
    def _():
        for k in range(2):
            halo_up(k).start()

    @pl.when(az > 0)
    def _():
        for k in range(2):
            halo_down(k).start()

    block = 32
    blocks = n_az * bins // block
    per = bins // block
    row = iota((16, F), 0)
    shift = jnp.zeros((16, F), jnp.int32)
    for s in range(1, n_az):
        shift = shift + (row >= s * per).astype(jnp.int32)
    inner = row - shift * per
    target = az + shift
    target = jnp.where(target >= n_az, target - n_az, target)
    starts = (target * 2 + fq) * bins + inner * block
    wide = slice(0, F)
    highc[0:16, wide], highs[0:16, wide] = small_trig(starts * iota((16, F), 1), F)
    lowc[:, wide], lows[:, wide] = small_trig(iota((block, F), 0) * iota((block, F), 1), F)

    @pl.loop(0, blocks)
    def _(i):
        hc, hs = highc[pl.ds(i, 1), wide], highs[pl.ds(i, 1), wide]
        lc, ls = lowc[:, wide], lows[:, wide]
        at = pl.ds(pl.multiple_of(i * block, block), block)
        rtab[at, :] = (hc * lc - hs * ls).astype(jnp.bfloat16)
        at = pl.ds(pl.multiple_of((blocks + i) * block, block), block)
        rtab[at, :] = (hs * lc + hc * ls).astype(jnp.bfloat16)

    for load in loads:
        load.wait()

    @pl.loop(0, parts * steps)
    def _(i):
        g = i // steps
        rows = pl.ds(pl.multiple_of(lax.rem(i, steps) * GROUP, GROUP), GROUP)
        lanes = lane_block(g, LANES)
        rel = offv[rows, lanes] + HW
        cnt = cntv[rows, lanes]
        zero = jnp.zeros(rel.shape, jnp.float32)
        taps = [
            jnp.where(t < cnt, tapv[t, rows, lanes].astype(jnp.float32), zero)
            for t in range(KT)
        ]
        for bit in range(4):
            step = 1 << bit
            on = (rel & step) != 0
            size = min(TAPS, len(taps) + step)
            taps = [
                jnp.where(
                    on,
                    taps[d - step] if d >= step else zero,
                    taps[d] if d < len(taps) else zero,
                )
                for d in range(size)
            ]
        for d in range(TAPS):
            wt[d, g, rows, :] = taps[d].astype(jnp.bfloat16)

    def wait_halo(k):
        @pl.when(az > 0)
        def _():
            halo_up(k).wait_recv()

        @pl.when(az < n_az - 1)
        def _():
            halo_down(k).wait_recv()

    def interpolate(c):
        slot = lax.rem(c, SLOTS)
        polar_copy(c).wait()

        @pl.when(c == 0)
        def _():
            wait_halo(0)

        @pl.when(c == FIRST)
        def _():
            wait_halo(1)

        for p in range(2):
            for g in range(parts):
                lanes = slice(g * LANES, (g + 1) * LANES)
                buf[p, g, 0:HW, :] = hl[p, c, :, lanes].astype(jnp.float32)
                buf[p, g, HW : HW + cols, :] = pv[slot, p, :, lanes].astype(jnp.float32)
                buf[p, g, HW + cols :, :] = hr[p, c, :, lanes].astype(jnp.float32)

        @pl.loop(0, parts * steps)
        def _(i):
            g = i // steps
            base = pl.multiple_of(lax.rem(i, steps) * GROUP, GROUP)
            lanes = lane_block(fq * parts + g, LANES)
            weights = [
                wt[d, g, pl.ds(base, GROUP), :].astype(jnp.float32) for d in range(TAPS)
            ]
            for p in range(2):
                acc = [None, None]
                for o in range(TAPS + 8):
                    cell = buf[p, g, pl.ds(base + o, 8), :]
                    for v in range(2):
                        d = o - 8 * v
                        if 0 <= d < TAPS:
                            term = weights[d][8 * v : 8 * v + 8] * cell
                            acc[v] = term if acc[v] is None else acc[v] + term
                value = jnp.concatenate(acc, axis=0).astype(jnp.bfloat16)
                xs[c, p, pl.ds(base, GROUP), lanes] = value

        fq_copy(c, lane_block(fq, freqs)).start()

        @pl.when(c + SLOTS < cuts)
        def _():
            polar_copy(c + SLOTS).start()

    def range_step(c):
        fq_copy(c, lane_block(1 - fq, freqs)).wait_recv()
        dims = (((1,), (1,)), ((), ()))
        table = rtab[...]
        fr = lax.dot_general(table, xs[c, 0], dims, preferred_element_type=jnp.float32)
        fi = lax.dot_general(table, xs[c, 1], dims, preferred_element_type=jnp.float32)
        half = n_az * bins
        scale = 1.0 / math.sqrt(F)
        real = ((fr[:half] - fi[half:]) * scale).astype(jnp.bfloat16)
        imag = ((fr[half:] + fi[:half]) * scale).astype(jnp.bfloat16)
        b, k = c // BATCH, lax.rem(c, BATCH)
        for p, part in enumerate((real, imag)):
            for s in range(n_az):
                piece = part[s * bins : s * bins + late]
                if s == 0:
                    zl[b, p, k, :, own_cols] = piece
                else:
                    rl[c, s - 1, p] = piece
                for g in range(early_groups):
                    at = s * bins + late + g * GROUP
                    er[g, 0, c, p, s] = part[at : at + GROUP]
        for core, shifts in enumerate((order[1:] + order[:1], order)):

            @pl.when(fq == core)
            def _():
                for s in shifts:
                    zl_copy(c, s, own_cols).start()

        for g in range(early_groups - 1):
            xe_copy(c, g).start()

        @pl.when(c < AHEAD)
        def _():
            xe_copy(c, early_groups - 1).start()

    order = list(range(1, n_az))

    def azimuth_tables():
        col = iota((block, A), 1)
        lowc[...], lows[...] = small_trig(iota((block, A), 0) * col, A)
        highc[...], highs[...] = small_trig(iota((A // block, A), 0) * block * col, A)

        @pl.loop(0, A // block)
        def _(i):
            hc, hs = highc[pl.ds(i, 1), :], highs[pl.ds(i, 1), :]
            at = pl.ds(pl.multiple_of(i * block, block), block)
            cos_a[at, :] = (hc * lowc[...] - hs * lows[...]).astype(jnp.bfloat16)
            sin_a[at, :] = (hs * lowc[...] + hc * lows[...]).astype(jnp.bfloat16)

    def height_tables():
        rows, width = 2 * heights, 4 * cuts
        row, col = iota((rows, 128), 0), iota((rows, 128), 1)
        out_imag = row >= heights
        height = el * heights + jnp.where(out_imag, row - heights, row)
        other = col >= 2 * cuts
        inner = jnp.where(other, col - 2 * cuts, col)
        in_imag = (inner & 1) == 1
        source = jnp.where(other, 1 - el, el)
        elev = source * cuts + (inner >> 1)
        cos_e, sin_e = small_trig(height * elev, E)
        sign = jnp.where(out_imag, sin_e, -sin_e)
        small = jnp.where(out_imag == in_imag, cos_e, sign)
        small = jnp.where(col < width, small, 0.0).astype(jnp.bfloat16)
        tall = rows * GROUP
        take_row = (iota((tall, rows), 0) // GROUP == iota((tall, rows), 1)).astype(
            jnp.bfloat16
        )
        mid = jnp.dot(take_row, small, preferred_element_type=jnp.float32)
        mid = mid.astype(jnp.bfloat16)

        @pl.loop(0, width * GROUP // TILE)
        def _(i):
            shape = (128, TILE)
            col_at = iota(shape, 1) + i * TILE
            take_col = (iota(shape, 0) == col_at // GROUP).astype(jnp.bfloat16)
            spread = jnp.dot(mid, take_col, preferred_element_type=jnp.float32)
            shape = (tall, TILE)
            same = (iota(shape, 0) & (GROUP - 1)) == (iota(shape, 1) & (GROUP - 1))
            htab[:, lane_block(i, TILE)] = jnp.where(same, spread, 0.0).astype(jnp.bfloat16)

    def cross_tile(left, t):
        rows = left.shape[0] // 2
        scale = 1.0 / math.sqrt(A)
        by_cos = jnp.dot(left, cos_a[:, lane_block(t, TILE)], preferred_element_type=jnp.float32)
        by_sin = jnp.dot(left, sin_a[:, lane_block(t, TILE)], preferred_element_type=jnp.float32)
        real = ((by_cos[:rows] - by_sin[rows:]) * scale).astype(jnp.bfloat16)
        imag = ((by_sin[:rows] + by_cos[rows:]) * scale).astype(jnp.bfloat16)
        return real, imag

    def cross_late(b):
        for k in range(BATCH):
            for s in order:
                zl_copy(b * BATCH + k, s, from_az(s)).wait_recv()

        @pl.loop(0, A // TILE)
        def _(t):
            left = zl[b].reshape(2 * BATCH * late, A)
            for p, part in enumerate(cross_tile(left, t)):
                part = part.reshape(BATCH, LATE, GROUP, TILE)
                for g in range(LATE):
                    span = pl.ds(b * BATCH, BATCH)
                    ch[g, 0, span, p, :, lane_block(t, TILE)] = part[:, g]

    def early_heights(g):
        for c in range(cuts):
            xe_copy(c, g).wait_recv()

        @pl.loop(0, n_az)
        def _(s):
            data = er[g, :, :, :, s].reshape(4 * cuts * GROUP, cols)
            total = jnp.dot(htab[...], data, preferred_element_type=jnp.float32)
            total = (total * (1.0 / math.sqrt(E))).astype(jnp.bfloat16)
            total = total.reshape(2, heights, GROUP, cols)

            @pl.when(s == 0)
            def _():
                ez[g, :, :, :, own_cols] = total

            @pl.when(s > 0)
            def _():
                eh[g, s - 1] = total

        for q in range(SPLIT):
            for s in order:
                ze_copy(g, q, s, own_cols).start()

    def cross_early(g, q):
        for s in order:
            ze_copy(g, q, s, from_az(s)).wait_recv()
        some = heights // SPLIT

        @pl.loop(0, A // TILE)
        def _(t):
            left = ez[g, :, q * some : (q + 1) * some].reshape(2 * some * GROUP, A)
            for p, part in enumerate(cross_tile(left, t)):
                at = late + g * GROUP
                out[p, q * some : (q + 1) * some, at : at + GROUP, lane_block(t, TILE)] = (
                    part.reshape(some, GROUP, TILE)
                )

    def late_heights(g, k):
        if g == 0 and k == 0:
            for b in range(batches // 2):
                xa_copy(b).wait_recv()
        for b in range(batches // 2, batches):
            xb_copy(b, g, k).wait_recv()
        some = A // TILE // HALVES

        @pl.loop(k * some, (k + 1) * some)
        def _(t):
            at = lane_block(t, TILE)
            data = ch[g, :, :, :, :, at].reshape(4 * cuts * GROUP, TILE)
            total = jnp.dot(htab[...], data, preferred_element_type=jnp.float32)
            total = (total * (1.0 / math.sqrt(E))).astype(jnp.bfloat16)
            out[:, :, g * GROUP : (g + 1) * GROUP, at] = total.reshape(2, heights, GROUP, TILE)

    def front(first, last):
        @pl.loop(first, last)
        def _(c):
            @pl.when(c < cuts)
            def _():
                interpolate(c)

            @pl.when(c > 0)
            def _():
                range_step(c - 1)

    front(0, cuts + 1)
    for c in range(AHEAD, cuts):
        xe_copy(c, early_groups - 1).start()
    height_tables()
    early_heights(0)
    azimuth_tables()
    cross_late(0)
    xa_copy(0).start()
    cross_late(1)
    xa_copy(1).start()
    for g in range(1, early_groups):
        early_heights(g)
    for b in range(batches // 2, batches):
        cross_late(b)
    for g in range(LATE):
        for k in range(HALVES):
            for b in range(batches // 2, batches):
                xb_copy(b, g, k).start()
    cross_early(0, 0)
    cross_early(0, 1)
    cross_early(1, 0)
    late_heights(0, 0)
    late_heights(0, 1)
    cross_early(1, 1)
    late_heights(1, 0)
    late_heights(1, 1)
    cross_early(2, 0)
    late_heights(2, 0)
    cross_early(2, 1)
    late_heights(2, 1)

    @pl.when(az < n_az - 1)
    def _():
        for k in range(2):
            halo_up(k).wait_send()

    @pl.when(az > 0)
    def _():
        for k in range(2):
            halo_down(k).wait_send()

    @pl.loop(0, cuts)
    def _(c):
        fq_copy(c, lane_block(fq, freqs)).wait_send()
        for s in order:
            zl_copy(c, s, own_cols).wait_send()
        for g in range(early_groups):
            xe_copy(c, g).wait_send()

    for g in range(early_groups):
        for q in range(SPLIT):
            for s in order:
                ze_copy(g, q, s, own_cols).wait_send()
    for b in range(batches // 2):
        xa_copy(b).wait_send()
    for b in range(batches // 2, batches):
        for g in range(LATE):
            for k in range(HALVES):
                xb_copy(b, g, k).wait_send()


def fused(polar, band_offset, tap_count, tap_weight):
    _, cuts, cols, freqs = polar.shape
    n_az = lax.axis_size("az")
    bins = F // (2 * n_az)
    late = LATE * GROUP
    heights = E // 2
    parts = freqs // LANES
    groups = (bins - late) // GROUP
    batches = cuts // BATCH
    far = n_az - 1
    half = jnp.bfloat16
    vmem = pltpu.VMEM
    dma = pltpu.SemaphoreType.DMA
    return pl.pallas_call(
        fused_body,
        out_shape=pltpu.VMEM((2, heights, bins, A), half),
        in_specs=[pl.BlockSpec(memory_space=pl.ANY)] * 4,
        out_specs=pl.BlockSpec(memory_space=pltpu.VMEM),
        scratch_shapes=[
            vmem((cuts, 2, cols, F), half),
            vmem((2, parts, cols + 2 * HW, LANES), jnp.float32),
            vmem((SLOTS, 2, cols, freqs), half),
            vmem((TAPS, parts, cols, LANES), half),
            vmem((cols, freqs), jnp.int32),
            vmem((cols, freqs), jnp.int32),
            vmem((KT, cols, freqs), half),
            vmem((2, cuts, HW, freqs), half),
            vmem((2, cuts, HW, freqs), half),
            vmem((32, A), jnp.float32),
            vmem((32, A), jnp.float32),
            vmem((32, A), jnp.float32),
            vmem((32, A), jnp.float32),
            vmem((2 * n_az * bins, F), half),
            vmem((A, A), half),
            vmem((A, A), half),
            vmem((2 * heights * GROUP, 4 * cuts * GROUP), half),
            vmem((cuts, far, 2, late, cols), half),
            vmem((batches, 2, BATCH, late, A), half),
            vmem((groups, 2, cuts, 2, n_az, GROUP, cols), half),
            vmem((groups, far, 2, heights, GROUP, cols), half),
            vmem((groups, 2, heights, GROUP, A), half),
            vmem((LATE, 2, cuts, 2, GROUP, A), half),
            dma((3,)),
            dma((SLOTS,)),
            dma((2, 2)),
            dma((2, 2)),
            dma((cuts,)),
            dma((cuts,)),
            dma((cuts, far)),
            dma((cuts, far)),
            dma((cuts, groups)),
            dma((cuts, groups)),
            dma((groups, SPLIT, far)),
            dma((groups, SPLIT, far)),
            dma((batches // 2,)),
            dma((batches // 2,)),
            dma((batches // 2, LATE, HALVES)),
            dma((batches // 2, LATE, HALVES)),
        ],
        compiler_params=pltpu.CompilerParams(
            collective_id=0, has_side_effects=True, vmem_limit_bytes=60000000
        ),
        name="image",
    )(polar, band_offset, tap_count, tap_weight)


def pick(polar, band_offset, tap_count, tap_weight):
    _, e_here, col_count, freq_count = polar.shape
    az_count = lax.axis_size("az")
    bins = F // (lax.axis_size("fq") * az_count)
    fits = (
        lax.axis_size("fq") == 2
        and lax.axis_size("el") == 2
        and az_count == 4
        and e_here == 4 * BATCH
        and bins == (LATE + EARLY) * GROUP
        and col_count == TILE
        and freq_count % LANES == 0
    )
    run = fused if fits else on_device
    return run(polar, band_offset, tap_count, tap_weight)


def solution(mesh):
    in_specs = (
        P(None, ("grp", "el"), "az", "fq"),
        P("az", "fq"),
        P("az", "fq"),
        P(None, "az", "fq"),
    )
    out_specs = P(None, ("grp", "el"), ("az", "fq"), None)
    return jax.shard_map(
        pick, mesh=mesh, in_specs=in_specs, out_specs=out_specs, check_vma=False
    )
```
